256 devices in a mesh: req: 32 (over z, x), row: 2 (over core), col: 4 (over y).
Axes of the slice: x: 4, y: 4, z: 8, core: 2. Of those that a mesh axis runs over, the one named last changes fastest.
Arguments:
- tokens: bfloat16 [32768, 1024], P(('req', 'row'), 'col'), may hold values from -6 to 6
- w_proj: bfloat16 [1024, 8, 512], P('col', 'row'), may hold values from -0.1875 to 0.1875
- adapter_a: bfloat16 [64, 1024, 16], P('req'), may hold values from -0.1875 to 0.1875
- adapter_b: bfloat16 [64, 16, 8, 256], P('req', None, 'row'), may hold values from -0.8984375 to 0.8984375
- adapter_row: int32 [64], replicated, may hold values from 0 to 63, each once
- adapter_of: int32 [32, 2], replicated, may hold values from 0 to 63
- len_blocks: int32 [32, 2], replicated, may hold values from 1 to 12, 16 in all within a row
- state_slot: int32 [64], replicated, may hold values from 0 to 63, as said below
- init_state: float32 [64, 8, 128, 128], P('req', 'row'), may hold values from -3 to 3
- decay: float32 [512, 8], P(('req', 'col'), 'row'), may hold values from 0 to 1, as said below
Outputs:
- memory_out: bfloat16 [32768, 1024], P(('req', 'col'), 'row')
The draws below stay inside these ranges and needn't reach their ends.
Inputs may be any that keep to these rules, and one draw needn't show every extreme that they name: `len_blocks`: each row sums to 16. `state_slot`: a permutation of the slots; slots k * 2 to (k + 1) * 2 - 1 are those of req index k. The 2 requests of req index g take one slot of req index (g - 1) mod 32 and one of req index (g - 16) mod 32, in an order and at positions within those indices that vary by draw. `decay`: every factor is above 0 and at most 1.
All inputs are finite; a program needn't handle non-finite values.
Results may differ from the reference program's by a relative error of at most 0.0062.
Values may be sent and summed in bfloat16 or wider, within the bound.
A program may use at most 128 MiB of HBM per device.

```python
import math
import jax
import jax.numpy as jnp
import numpy as np
from jax import lax

D = 1024
H = 8
HD = 128
RANK = 16
NADP = 64
BLK = 64
REQ_GRP = 2
GROUP_TOK = 1024
TOKENS = 32768
REQS = 64
N_REQ = 32


def draw_state_slot(key, part):
    random_key_list = jax.random.split(jax.random.fold_in(key, 17), 2)
    base_offsets = jnp.array([1, N_REQ // 2], dtype=jnp.int32)
    order = jax.random.permutation(random_key_list[0], 2).astype(jnp.int32)
    offsets = base_offsets[order][:REQ_GRP]
    within = jax.random.permutation(random_key_list[1], REQ_GRP).astype(jnp.int32)
    groups = jnp.arange(N_REQ, dtype=jnp.int32)[:, None]
    owner = (groups - offsets[None, :]) % N_REQ
    return (owner * REQ_GRP + within[None, :]).reshape(REQS).astype(jnp.int32)


def draw_decay(key, part):
    random_key_list = jax.random.split(key, 6)
    memory_sequence = GROUP_TOK // BLK
    array_dimensions = (TOKENS // BLK, H)
    slow = jax.random.uniform(random_key_list[0], (H,)) < 0.5
    random_noise = jnp.exp(jax.random.uniform(random_key_list[1], array_dimensions, minval=-0.69, maxval=0.69))
    keep_chain = jax.random.uniform(random_key_list[2], (H,), minval=0.3, maxval=0.6)
    slow_log = jnp.log(keep_chain) / memory_sequence
    reach = jax.random.uniform(random_key_list[3], (H,), minval=30.0, maxval=50.0)
    fast_log = -1.0 * BLK / reach
    decay_rates = jnp.where(slow, slow_log, fast_log)
    spike_factor = jax.random.uniform(random_key_list[4], array_dimensions) < 3.0 / memory_sequence
    split_boundary = jax.random.uniform(random_key_list[5], array_dimensions, minval=0.5, maxval=0.8)
    return jnp.exp(decay_rates[None, :] * random_noise) * jnp.where(spike_factor, split_boundary, 1.0)


def with_ends(drawn, key, least, top_value):
    extent = drawn.shape
    index_at = [jax.random.randint(jax.random.fold_in(key, axis), (), 0, extent[axis]) for axis in range(len(extent))]
    drawn = drawn.at[tuple(index_at)].set(least)
    longest = extent.index(max(extent))
    index_at[longest] = (index_at[longest] + 1) % extent[longest]
    return drawn.at[tuple(index_at)].set(top_value)


def block_scale(key, shape, cuts, low, top_value):
    factor_of = 1.0
    for dim, blocks in cuts:
        draws = jax.random.uniform(jax.random.fold_in(jax.random.fold_in(key, 6), dim), (blocks,), jnp.float32, low / len(cuts), top_value / len(cuts))
        factor_of = factor_of * jnp.repeat(jnp.exp(draws), shape[dim] // blocks).reshape((-1,) + (1,) * (len(shape) - 1 - dim))
    return factor_of


def profile(count, total, most, slope):
    portions = [(1 << 20) // math.isqrt(grade ** slope) + 1 for grade in range(2, count + 1)]
    rest, counts = total - most - (count - 1), [1] * (count - 1)
    while rest > 0:
        candidates = [i for i in range(count - 1) if counts[i] < most]
        mass, remaining = sum([portions[i] for i in candidates]), rest
        for i in candidates:
            more = min(most - counts[i], max(1, remaining * portions[i] // mass), rest)
            counts[i] = counts[i] + more
            rest = rest - more
    return np.array([most] + counts)


def ragged(stream_key, amount, total, most, lean):
    if amount == 2:
        one = jax.random.randint(stream_key, (), max(1, total - most), min(most, total - 1) + 1)
        return jnp.stack([one, total - one])
    sizes = jnp.asarray(profile(amount, total, most, lean), jnp.int32)
    couples = (amount - 1) // 2
    donor, receiver = sizes[1:1 + 2 * couples:2], sizes[2:2 + 2 * couples:2]
    room = jnp.minimum(donor - 1, most - receiver)
    shifted = jax.random.randint(jax.random.fold_in(stream_key, 1), (couples,), 0, 1 << 20) % (room + 1)
    sizes = sizes.at[1:1 + 2 * couples:2].set(donor - shifted).at[2:2 + 2 * couples:2].set(receiver + shifted)
    return sizes[jax.random.permutation(jax.random.fold_in(stream_key, 2), amount)]


def normal_values(rng, shape, scale, bound, cuts=(), kind=jnp.bfloat16):
    values = scale * jax.random.normal(rng, shape, jnp.float32)
    if cuts:
        values = values * block_scale(rng, shape, cuts, -0.22, 0.18)
    return jnp.clip(values, -bound, bound).astype(kind)


def setup_inputs(seed: int = 0) -> dict:
    key_of = jax.random.split(jax.random.key(seed), 11)
    tokens = normal_values(key_of[0], (TOKENS, D), 1.0, 6.0, ((0, 64), (1, 4)))
    w_proj = normal_values(key_of[1], (D, H, 4 * HD), D ** -0.5, 0.1875, ((0, 4), (1, 2)))
    adapter_a = normal_values(key_of[2], (NADP, D, RANK), D ** -0.5, 0.1875, ((0, 32),))
    adapter_b = normal_values(key_of[3], (NADP, RANK, H, 2 * HD), 0.15, 0.8984375, ((0, 32), (2, 2)))
    adapter_row = jax.random.permutation(key_of[4], NADP).astype(jnp.int32)
    adapter_of = with_ends(jax.random.randint(key_of[5], (N_REQ, REQ_GRP), 0, NADP), jax.random.fold_in(key_of[5], 1), 0, NADP - 1).astype(jnp.int32)
    len_blocks = jax.vmap(lambda own: ragged(own, REQ_GRP, GROUP_TOK // BLK, GROUP_TOK // BLK * 3 // 4, 2))(jax.random.split(key_of[6], N_REQ)).reshape((N_REQ, REQ_GRP)).astype(jnp.int32)
    state_slot = draw_state_slot(jax.random.fold_in(key_of[10], 71), 0)
    init_state = normal_values(key_of[8], (REQS, H, HD, HD), 0.5, 3.0, ((0, 32), (1, 2)), jnp.float32)
    decay = draw_decay(jax.random.fold_in(key_of[10], 71), 0)
    return {"tokens": tokens, "w_proj": w_proj, "adapter_a": adapter_a, "adapter_b": adapter_b, "adapter_row": adapter_row, "adapter_of": adapter_of, "len_blocks": len_blocks, "state_slot": state_slot, "init_state": init_state, "decay": decay}


def unit(values):
    scale = lax.rsqrt(lax.optimization_barrier(jnp.mean(values * values, axis=-1, keepdims=True)) + 1e-06)
    return values * scale / math.sqrt(values.shape[-1])

def block_info(lengths, block_ids):
    lengths = lengths.astype(jnp.int32)
    starts = (jnp.cumsum(lengths) - lengths).astype(jnp.int32)
    is_start = jnp.any(block_ids[:, None] == starts[None, :], axis=1)
    request = (lax.optimization_barrier(jnp.sum((block_ids[:, None] >= starts[None, :]).astype(jnp.int32), axis=1)) - 1).astype(jnp.int32)
    return (is_start, request)

def add_adapter(base_part, delta):
    return jnp.stack([base_part[:, :, 0] + delta[:, :, 0], base_part[:, :, 1], base_part[:, :, 2] + delta[:, :, 1], base_part[:, :, 3]], axis=2)

def reference(tokens, w_proj, adapter_a, adapter_b, adapter_row, adapter_of, len_blocks, state_slot, init_state, decay):
    highest = lax.Precision.HIGHEST
    nblk = GROUP_TOK // BLK
    w_flat = w_proj.reshape(D, H * 4 * HD)
    groups = tokens.reshape(N_REQ, GROUP_TOK, D)
    decays = decay.reshape(N_REQ, nblk, H)
    causal = jnp.tril(jnp.ones((BLK, BLK), jnp.float32))

    def one_group(inputs):
        inputs_x, group_id, fades = inputs
        block_ids = jnp.arange(nblk, dtype=jnp.int32)
        is_start, request = block_info(len_blocks[group_id], block_ids)
        tok_req = jnp.repeat(request, BLK)
        onehot = (tok_req[:, None] == jnp.arange(REQ_GRP, dtype=jnp.int32)[None, :]).astype(jnp.float32)
        picked = adapter_row[adapter_of[group_id]]
        a_stack = jnp.transpose(adapter_a[picked], (1, 0, 2)).reshape(D, REQ_GRP * RANK)
        b_stack = adapter_b[picked].reshape(REQ_GRP * RANK, H * 2 * HD).astype(jnp.float32)
        lowrank = jnp.dot(inputs_x, a_stack, preferred_element_type=jnp.float32).reshape(GROUP_TOK, REQ_GRP, RANK)
        lowrank = (lowrank * onehot[:, :, None]).reshape(GROUP_TOK, REQ_GRP * RANK)
        delta = jnp.dot(lowrank, b_stack, precision=highest).reshape(GROUP_TOK, H, 2, HD)
        projected = jnp.dot(inputs_x, w_flat, preferred_element_type=jnp.float32).reshape(GROUP_TOK, H, 4, HD)
        parts = add_adapter(projected, delta).astype(jnp.bfloat16)
        query = unit(parts[:, :, 0].astype(jnp.float32)).reshape(nblk, BLK, H, HD)
        keys_n = unit(parts[:, :, 1].astype(jnp.float32)).reshape(nblk, BLK, H, HD)
        values = parts[:, :, 2].astype(jnp.float32).reshape(nblk, BLK, H, HD)
        slots = state_slot[group_id * REQ_GRP + request]

        def step(state, blocks):
            q_block, k_block, v_block, fade, start_here, slot = blocks
            state = jnp.where(start_here, init_state[slot], state)
            read = jnp.einsum('thd,hde->the', q_block, state, precision=highest)
            scores = jnp.einsum('thd,shd->hts', q_block, k_block, precision=highest) * causal[None]
            inner = jnp.einsum('hts,she->the', scores, v_block, precision=highest)
            update = jnp.einsum('thd,the->hde', k_block, v_block, precision=highest) / BLK
            return (fade[:, None, None] * state + update, read + inner)
        start_state = jnp.zeros((H, HD, HD), jnp.float32)
        _, mem = lax.scan(step, start_state, (query, keys_n, values, fades, is_start, slots))
        gate_part = parts[:, :, 3].astype(jnp.float32)
        result = jax.nn.sigmoid(gate_part) * mem.reshape(GROUP_TOK, H, HD)
        return result.reshape(GROUP_TOK, H * HD).astype(jnp.bfloat16)
    outputs = lax.map(one_group, (groups, jnp.arange(N_REQ, dtype=jnp.int32), decays))
    return outputs.reshape(TOKENS, H * HD)
```

```python
import functools
import math

import jax
import jax.numpy as jnp
from jax import lax
from jax.experimental import pallas as pl
from jax.experimental.pallas import tpu as pltpu
from jax.sharding import PartitionSpec as P

BLK = 64
NX = 4
NY = 4
MESH = pl.DeviceIdType.MESH
F32 = jnp.float32
BF16 = jnp.bfloat16


def kernel(
    n_req,
    row_ref,
    of_ref,
    len_ref,
    slot_ref,
    tok_ref,
    w_ref,
    a_ref,
    b_ref,
    state_ref,
    decay_ref,
    out_ref,
    tok,
    w,
    za,
    zb,
    xsa,
    xsb,
    xra,
    xrb,
    afull,
    bfull,
    bh,
    states,
    dec,
    carry,
    osend,
    tok_s,
    tok_r,
    w_s,
    w_r,
    z_s,
    z_r,
    x_s,
    x_r,
    g_s,
    g_r,
    st_s,
    st_r,
    d_s,
    d_r,
    o_s,
    o_r,
    loc,
):
    nz = n_req // NX
    g = lax.axis_index("req")
    r = lax.axis_index("row")
    c = lax.axis_index("col")
    z, x = g // NX, lax.rem(g, NX)
    sib = 1 - r
    right, left, opp = lax.rem(c + 1, NY), lax.rem(c + 3, NY), lax.rem(c + 2, NY)
    half = tok_ref.shape[0]
    part = half // 2
    base = r * half

    def rem_copy(src, dst, ssem, rsem, dev):
        return pltpu.make_async_remote_copy(
            src_ref=src, dst_ref=dst, send_sem=ssem, recv_sem=rsem, device_id=dev, device_id_type=MESH
        )

    def at_z(d):
        return {"req": lax.rem(z + d, nz) * NX + x}

    def at_x(d):
        return {"req": z * NX + lax.rem(x + d, NX)}

    def at_g(d):
        return {"req": lax.rem(g + d, n_req)}

    group = [(dr, dc) for dr in range(2) for dc in range(NY) if dr or dc]

    def in_group(dr, dc):
        return {"row": lax.rem(r + dr, 2), "col": lax.rem(c + dc, NY)}

    barrier = pltpu.get_barrier_semaphore()
    partners = [in_group(*p) for p in group]
    partners += [at_z(d) for d in range(1, nz)] + [at_x(d) for d in range(1, NX)]
    partners += [at_g(1), at_g(n_req - 1)]
    for dev in partners:
        pl.semaphore_signal(barrier, inc=1, device_id=dev, device_id_type=MESH)
    pl.semaphore_wait(barrier, len(partners))

    f = 2 * c + r
    fa = pl.multiple_of(f * 128, 128)
    mine_a = a_ref.at[:, :, pl.ds(fa, 128)]
    mine_b = b_ref.at[:, pl.ds(4 * c, 4)]
    sends = []
    z_in = []
    for d in range(1, nz):
        for k, (src, dst) in enumerate(((mine_a, za), (mine_b, zb))):
            cp = rem_copy(src, dst.at[pl.ds(2 * z, 2)], z_s.at[k, d], z_r.at[k, d], at_z(d))
            cp.start()
            sends.append(cp)
            zo = lax.rem(z + nz - d, nz)
            slot = dst.at[pl.ds(2 * zo, 2)]
            z_in.append(rem_copy(src, slot, z_s.at[k, d], z_r.at[k, d], at_z(d)))
    own_a = pltpu.make_async_copy(mine_a, za.at[pl.ds(2 * z, 2)], loc.at[0])
    own_b = pltpu.make_async_copy(mine_b, zb.at[pl.ds(2 * z, 2)], loc.at[1])
    own_a.start()
    own_b.start()

    w_in = []
    for k, (to, frm) in enumerate(((right, left), (left, right), (opp, opp))):
        cp = rem_copy(w_ref.at[to], w.at[c], w_s.at[k], w_r.at[k], {"col": to})
        cp.start()
        sends.append(cp)
        w_in.append(rem_copy(w_ref.at[to], w.at[frm], w_s.at[k], w_r.at[k], {"col": to}))
    own_w = pltpu.make_async_copy(w_ref.at[c], w.at[c], loc.at[2])
    own_w.start()

    def chunk(k):
        return pl.ds(base + k * part, part)

    def tsend(i, src, dst, dev):
        cp = rem_copy(src, dst, tok_s.at[i], tok_r.at[i], dev)
        cp.start()
        sends.append(cp)

    def twait(i, slot, dev):
        rem_copy(slot, slot, tok_s.at[i], tok_r.at[i], dev).wait_recv()

    for i, (to, k) in enumerate(((right, 0), (left, 1), (right, 1), (left, 0))):
        tsend(i, tok_ref.at[pl.ds(k * part, part)], tok.at[c, chunk(k)], {"col": to})
    tsend(4, tok_ref, tok.at[c, pl.ds(base, half)], {"row": sib})
    own_t = pltpu.make_async_copy(tok_ref, tok.at[c, pl.ds(base, half)], loc.at[3])
    own_t.start()

    d_in = []
    for d in range(1, NY):
        to, frm = lax.rem(c + d, NY), lax.rem(c + NY - d, NY)
        cp = rem_copy(decay_ref, dec.at[c], d_s.at[d], d_r.at[d], {"col": to})
        cp.start()
        sends.append(cp)
        d_in.append(rem_copy(decay_ref, dec.at[frm], d_s.at[d], d_r.at[d], {"col": to}))
    own_d = pltpu.make_async_copy(decay_ref, dec.at[c], loc.at[4])
    own_d.start()
    st_in = []
    for k, d in enumerate((1, n_req // 2)):
        cp = rem_copy(state_ref.at[:, c], states.at[pl.ds(2 * k, 2)], st_s.at[k], st_r.at[k], at_g(d))
        cp.start()
        sends.append(cp)
        st_in.append(cp)

    slot_l0, slot_l1 = tok.at[left, chunk(0)], tok.at[left, chunk(1)]
    slot_r0, slot_r1 = tok.at[right, chunk(0)], tok.at[right, chunk(1)]
    slot_o0, slot_o1 = tok.at[opp, chunk(0)], tok.at[opp, chunk(1)]
    twait(0, slot_l0, {"col": right})
    tsend(5, slot_l0, slot_l0, {"col": right})
    tsend(6, slot_l0, slot_l0, {"row": sib})
    twait(1, slot_r1, {"col": left})
    tsend(7, slot_r1, slot_r1, {"col": left})
    tsend(8, slot_r1, slot_r1, {"row": sib})

    for cp in z_in:
        cp.wait_recv()
    own_a.wait()
    own_b.wait()
    for d in range(NX):
        gx = z * NX + lax.rem(x + d, NX)
        for j in range(2):
            p = row_ref[of_ref[j, gx]]
            idx = 2 * (p // (2 * NX)) + lax.rem(p, 2)
            if d == 0:
                xra[0, j] = za[idx]
                xrb[0, j] = zb[idx]
            else:
                xsa[d - 1, j] = za[idx]
                xsb[d - 1, j] = zb[idx]
    x_in = []
    for d in range(1, NX):
        for k, (src, dst) in enumerate(((xsa, xra), (xsb, xrb))):
            cp = rem_copy(src.at[d - 1], dst.at[d], x_s.at[k, d], x_r.at[k, d], at_x(d))
            cp.start()
            sends.append(cp)
            x_in.append(cp)

    twait(2, slot_l1, {"col": right})
    tsend(9, slot_l1, slot_l1, {"row": sib})
    twait(3, slot_r0, {"col": left})
    tsend(10, slot_r0, slot_r0, {"row": sib})

    for cp in x_in:
        cp.wait_recv()
    for j in range(2):
        p = row_ref[of_ref[j, g]]
        xo = lax.rem(p // 2, NX)
        dd = lax.rem(x - xo + NX, NX)
        afull[pl.ds(16 * j, 16), pl.ds(fa, 128)] = xra[dd, j]
        bfull[j, pl.ds(4 * c, 4)] = xrb[dd, j]
    g_in = []
    ga = afull.at[:, pl.ds(fa, 128)]
    for i, (dr, dc) in enumerate(group):
        cp = rem_copy(ga, ga, g_s.at[0, i], g_r.at[0, i], in_group(dr, dc))
        cp.start()
        sends.append(cp)
        rf = 2 * lax.rem(c + NY - dc, NY) + lax.rem(r + dr, 2)
        slot = afull.at[:, pl.ds(pl.multiple_of(rf * 128, 128), 128)]
        g_in.append(rem_copy(ga, slot, g_s.at[0, i], g_r.at[0, i], in_group(dr, dc)))
        if dr == 0:
            gb = bfull.at[:, pl.ds(4 * c, 4)]
            cp = rem_copy(gb, gb, g_s.at[1, i], g_r.at[1, i], in_group(dr, dc))
            cp.start()
            sends.append(cp)
            slot = bfull.at[:, pl.ds(4 * lax.rem(c + NY - dc, NY), 4)]
            g_in.append(rem_copy(gb, slot, g_s.at[1, i], g_r.at[1, i], in_group(dr, dc)))

    twait(5, slot_o0, {"col": right})
    tsend(11, slot_o0, slot_o0, {"row": sib})
    twait(7, slot_o1, {"col": left})
    tsend(12, slot_o1, slot_o1, {"row": sib})

    other = sib * half
    own_t.wait()
    own_w.wait()
    own_d.wait()
    for cp in w_in + d_in + st_in + g_in:
        cp.wait_recv()
    dev = {"row": sib}
    twait(4, tok.at[c, pl.ds(other, half)], dev)
    twait(6, tok.at[left, pl.ds(other, part)], dev)
    twait(8, tok.at[right, pl.ds(other + part, part)], dev)
    twait(9, tok.at[left, pl.ds(other + part, part)], dev)
    twait(10, tok.at[right, pl.ds(other, part)], dev)
    twait(11, tok.at[opp, pl.ds(other, part)], dev)
    twait(12, tok.at[opp, pl.ds(other + part, part)], dev)

    head_rows = lax.broadcasted_iota(jnp.int32, (4, 256), 0) == c
    for j in range(2):
        for k in range(16):
            row = jnp.sum(jnp.where(head_rows, bfull[j, k].astype(F32), 0.0), axis=0, keepdims=True)
            bh[pl.ds(16 * j + k, 1), :] = row

    first = len_ref[0, g]
    init = []
    for j in range(2):
        s = slot_ref[2 * g + j]
        far = jnp.where(s // 2 == lax.rem(g + n_req - 1, n_req), 0, 2)
        init.append(states[far + lax.rem(s, 2)])
    carry[0] = init[0]
    carry[1] = init[1]

    tile = 4 * BLK
    rows_i = lax.broadcasted_iota(jnp.int32, (tile, 1), 0)
    ti = lax.broadcasted_iota(jnp.int32, (tile, tile), 0)
    si = lax.broadcasted_iota(jnp.int32, (tile, tile), 1)
    seen = (ti // BLK == si // BLK) & (si <= ti)
    nt = (((1,), (1,)), ((), ()))
    tn = (((0,), (0,)), ((), ()))
    inv = 1.0 / math.sqrt(128.0)

    def one_tile(m, _):
        span = pl.ds(pl.multiple_of(m * tile, tile), tile)
        proj = jnp.zeros((tile, 512), F32)
        low = jnp.zeros((tile, 32), F32)
        for cc in range(NY):
            t = tok[cc, span, :]
            proj += jnp.dot(t, w[cc], preferred_element_type=F32)
            low += lax.dot_general(t, afull[:, cc * 256 : (cc + 1) * 256], nt, preferred_element_type=F32)
        request = (m * 4 + rows_i // BLK >= first).astype(jnp.int32)
        owner = lax.broadcasted_iota(jnp.int32, (tile, 32), 1) // 16
        low = jnp.where(owner == request, low, 0.0)
        hi = low.astype(BF16)
        lo = (low - hi.astype(F32)).astype(BF16)
        up = bh[...].astype(BF16)
        delta = jnp.dot(hi, up, preferred_element_type=F32) + jnp.dot(lo, up, preferred_element_type=F32)
        q = (proj[:, 0:128] + delta[:, 0:128]).astype(BF16)
        k = proj[:, 128:256].astype(BF16)
        v = (proj[:, 256:384] + delta[:, 128:256]).astype(BF16)
        gate = proj[:, 384:512].astype(BF16).astype(F32)
        qf, kf = q.astype(F32), k.astype(F32)
        sq = lax.rsqrt(jnp.mean(qf * qf, axis=1, keepdims=True) + 1e-06) * inv
        sk = lax.rsqrt(jnp.mean(kf * kf, axis=1, keepdims=True) + 1e-06) * inv
        vk = (v.astype(F32) * sk).astype(BF16)
        scores = lax.dot_general(q, k, nt, preferred_element_type=F32)
        scores = jnp.where(seen, scores, 0.0).astype(BF16)
        inner = jnp.dot(scores, vk, preferred_element_type=F32)
        dm = dec[m]
        fade = jnp.sum(
            jnp.where(lax.broadcasted_iota(jnp.int32, (4, 4), 1) == c, dm, 0.0), axis=1, keepdims=True
        )
        reads = []
        state = carry[0]
        for i in range(4):
            state = jnp.where(m * 4 + i == first, carry[1], state)
            sl = slice(i * BLK, (i + 1) * BLK)
            reads.append(jnp.dot(q[sl], state.astype(BF16), preferred_element_type=F32))
            upd = lax.dot_general(k[sl], vk[sl], tn, preferred_element_type=F32)
            state = state * fade[i : i + 1, :] + upd * (1.0 / BLK)
        carry[0] = state
        mem = (jnp.concatenate(reads, axis=0) + inner) * sq
        osend[m] = (mem * jax.nn.sigmoid(gate)).astype(BF16)

        place = out_ref.at[:, pl.ds(pl.multiple_of(c * 128, 128), 128)]

        @pl.when(m == c)
        def _():
            pltpu.make_async_copy(osend.at[m], place, loc.at[5]).start()

        @pl.when(m != c)
        def _():
            rem_copy(osend.at[m], place, o_s.at[m], o_r.at[c], {"col": m}).start()

        return 0

    lax.fori_loop(0, NY, one_tile, 0)

    for cp in sends:
        cp.wait_send()
    for d in range(1, NY):
        frm = lax.rem(c + d, NY)
        place = out_ref.at[:, pl.ds(pl.multiple_of(frm * 128, 128), 128)]
        cp = rem_copy(osend.at[frm], place, o_s.at[frm], o_r.at[frm], {"col": frm})
        cp.wait_send()
        cp.wait_recv()
    place = out_ref.at[:, pl.ds(pl.multiple_of(c * 128, 128), 128)]
    pltpu.make_async_copy(osend.at[c], place, loc.at[5]).wait()


def body(
    n_req, tokens, w_proj, adapter_a, adapter_b, adapter_row, adapter_of, len_blocks, state_slot, init_state, decay
):
    w_heads = jnp.transpose(w_proj, (1, 0, 2))
    a_t = jnp.swapaxes(adapter_a, 1, 2)
    nz = n_req // NX
    dma = pltpu.SemaphoreType.DMA
    smem = pl.BlockSpec(memory_space=pltpu.SMEM)
    anym = pl.BlockSpec(memory_space=pl.ANY)
    return pl.pallas_call(
        functools.partial(kernel, n_req),
        out_shape=jax.ShapeDtypeStruct((256, 512), BF16),
        in_specs=[smem] * 4 + [anym] * 5 + [pl.BlockSpec(memory_space=pltpu.VMEM)],
        out_specs=anym,
        scratch_shapes=[
            pltpu.VMEM((NY, 1024, 256), BF16),
            pltpu.VMEM((NY, 256, 512), BF16),
            pltpu.VMEM((2 * nz, 16, 128), BF16),
            pltpu.VMEM((2 * nz, 4, 4, 256), BF16),
            pltpu.VMEM((NX - 1, 2, 16, 128), BF16),
            pltpu.VMEM((NX - 1, 2, 4, 4, 256), BF16),
            pltpu.VMEM((NX, 2, 16, 128), BF16),
            pltpu.VMEM((NX, 2, 4, 4, 256), BF16),
            pltpu.VMEM((32, 1024), BF16),
            pltpu.VMEM((2, 16, 4, 256), BF16),
            pltpu.VMEM((32, 256), F32),
            pltpu.VMEM((4, 128, 128), F32),
            pltpu.VMEM((NY, 4, 4), F32),
            pltpu.VMEM((2, 128, 128), F32),
            pltpu.VMEM((NY, 256, 128), BF16),
            dma((13,)),
            dma((13,)),
            dma((3,)),
            dma((3,)),
            dma((2, nz)),
            dma((2, nz)),
            dma((2, NX)),
            dma((2, NX)),
            dma((2, 7)),
            dma((2, 7)),
            dma((2,)),
            dma((2,)),
            dma((NY,)),
            dma((NY,)),
            dma((NY,)),
            dma((NY,)),
            dma((6,)),
        ],
        compiler_params=pltpu.CompilerParams(collective_id=0, has_side_effects=True),
        name="memory_layer",
    )(
        adapter_row,
        jnp.transpose(adapter_of),
        jnp.transpose(len_blocks),
        state_slot,
        tokens,
        w_heads,
        a_t,
        adapter_b,
        init_state,
        decay,
    )


def solution(mesh):
    placed = (
        P(("req", "row"), "col"),
        P("col", "row", None),
        P("req", None, None),
        P("req", None, "row", None),
        P(),
        P(),
        P(),
        P(),
        P("req", "row", None, None),
        P(("req", "col"), "row"),
    )
    return jax.shard_map(
        functools.partial(body, mesh.shape["req"]),
        mesh=mesh,
        in_specs=placed,
        out_specs=P(("req", "col"), "row"),
        check_vma=False,
    )
```

```python
import functools
import math

import jax
import jax.numpy as jnp
from jax import lax
from jax.experimental import pallas as pl
from jax.experimental.pallas import tpu as pltpu
from jax.sharding import PartitionSpec as P

BLK = 64
NX = 4
NY = 4
MESH = pl.DeviceIdType.MESH
F32 = jnp.float32
BF16 = jnp.bfloat16


def kernel(
    n_req,
    row_ref,
    of_ref,
    len_ref,
    slot_ref,
    tok_ref,
    w_ref,
    a_ref,
    b_ref,
    state_ref,
    decay_ref,
    out_ref,
    tok,
    w,
    za,
    zb,
    xsa,
    xsb,
    xra,
    xrb,
    afull,
    bfull,
    bh,
    wtmp,
    acc,
    sloc,
    ssend,
    states,
    dec,
    carry,
    osend,
    tok_s,
    tok_r,
    w_s,
    w_r,
    z_s,
    z_r,
    x_s,
    x_r,
    g_s,
    g_r,
    st_s,
    st_r,
    d_s,
    d_r,
    o_s,
    o_r,
    loc,
    up_sem,
    down_sem,
    side_sem,
):
    nz = n_req // NX
    g = lax.axis_index("req")
    r = lax.axis_index("row")
    c = lax.axis_index("col")
    z, x = g // NX, lax.rem(g, NX)
    sib = 1 - r
    right, left, opp = lax.rem(c + 1, NY), lax.rem(c + 3, NY), lax.rem(c + 2, NY)
    half = tok_ref.shape[0]
    part = half // 2
    base = r * half

    def rem_copy(src, dst, ssem, rsem, dev):
        return pltpu.make_async_remote_copy(
            src_ref=src, dst_ref=dst, send_sem=ssem, recv_sem=rsem, device_id=dev, device_id_type=MESH
        )

    def at_z(d):
        return {"req": lax.rem(z + d, nz) * NX + x}

    def at_x(d):
        return {"req": z * NX + lax.rem(x + d, NX)}

    def at_g(d):
        return {"req": lax.rem(g + d, n_req)}

    group = [(dr, dc) for dr in range(2) for dc in range(NY) if dr or dc]

    def in_group(dr, dc):
        return {"row": lax.rem(r + dr, 2), "col": lax.rem(c + dc, NY)}

    near = [in_group(*p) for p in group] + [at_z(1), at_z(nz - 1), at_x(1), at_x(NX - 1)]
    barrier = pltpu.get_barrier_semaphore()
    for dev in near:
        pl.semaphore_signal(barrier, inc=1, device_id=dev, device_id_type=MESH)
    pl.semaphore_wait(barrier, len(near))

    sends = []

    def send(src, dst, ssem, rsem, dev):
        cp = rem_copy(src, dst, ssem, rsem, dev)
        cp.start()
        sends.append(cp)

    def landed(slot, ssem, rsem, dev):
        rem_copy(slot, slot, ssem, rsem, dev).wait_recv()

    hrow = lax.rem(x, 2) * 128
    orow = 128 - hrow
    eighth = 64

    def wsend(i, src, dst, dev):
        send(src, dst, w_s.at[i], w_r.at[i], dev)

    def wwait(i, slot, dev):
        landed(slot, w_s.at[i], w_r.at[i], dev)

    mine_h = pl.ds(hrow, 128)
    first_h, second_h = pl.ds(hrow, eighth), pl.ds(hrow + eighth, eighth)
    first_o, second_o = pl.ds(orow, eighth), pl.ds(orow + eighth, eighth)
    wsend(0, w_ref.at[opp, first_h], wtmp.at[0], {"col": right})
    wsend(1, w_ref.at[opp, second_h], wtmp.at[1], {"col": left})
    wsend(2, w_ref.at[right, mine_h], w.at[c, mine_h], {"col": right})
    wsend(3, w_ref.at[left, mine_h], w.at[c, mine_h], {"col": left})

    def chunk(k):
        return pl.ds(base + k * part, part)

    def tsend(i, src, dst, dev):
        send(src, dst, tok_s.at[i], tok_r.at[i], dev)

    def twait(i, slot, dev):
        landed(slot, tok_s.at[i], tok_r.at[i], dev)

    def tok_chunk(k):
        return tok_ref.at[pl.ds(k * part, part)]

    tsend(0, tok_chunk(0), tok.at[c, chunk(0)], {"col": right})
    tsend(1, tok_chunk(1), tok.at[c, chunk(1)], {"col": left})
    tsend(4, tok_ref, tok.at[c, pl.ds(base, half)], {"row": sib})
    own_t = pltpu.make_async_copy(tok_ref, tok.at[c, pl.ds(base, half)], loc.at[3])
    own_t.start()
    own_w = pltpu.make_async_copy(w_ref.at[c], w.at[c], loc.at[2])
    own_w.start()
    own_s = pltpu.make_async_copy(state_ref.at[:, c], sloc, loc.at[6])
    own_s.start()

    d_in = []
    for d in range(1, NY):
        to, frm = lax.rem(c + d, NY), lax.rem(c + NY - d, NY)
        send(decay_ref, dec.at[c], d_s.at[d], d_r.at[d], {"col": to})
        d_in.append((dec.at[frm], d_s.at[d], d_r.at[d], {"col": to}))
    own_d = pltpu.make_async_copy(decay_ref, dec.at[c], loc.at[4])
    own_d.start()

    for step in range(3):
        pl.semaphore_signal(up_sem, inc=1, device_id=at_z(nz - 1), device_id_type=MESH)
        pl.semaphore_signal(down_sem, inc=1, device_id=at_z(1), device_id_type=MESH)
        if step == 0:
            pl.semaphore_signal(side_sem, inc=1, device_id=at_x(NX - 1), device_id_type=MESH)
            pl.semaphore_wait(side_sem, 1)
        pl.semaphore_wait(up_sem, 1)
        pl.semaphore_wait(down_sem, 1)

    f = 2 * c + r
    fa = pl.multiple_of(f * 128, 128)
    mine_a = a_ref.at[:, :, pl.ds(fa, 128)]
    mine_b = b_ref.at[:, pl.ds(4 * c, 4)]
    z_in = []
    for d in (4, 3, 5, 2, 6, 1, 7):
        zo = lax.rem(z + nz - d, nz)
        for k, (src, dst) in enumerate(((mine_a, za), (mine_b, zb))):
            send(src, dst.at[pl.ds(2 * z, 2)], z_s.at[k, d], z_r.at[k, d], at_z(d))
            z_in.append((dst.at[pl.ds(2 * zo, 2)], z_s.at[k, d], z_r.at[k, d], at_z(d)))
    own_a = pltpu.make_async_copy(mine_a, za.at[pl.ds(2 * z, 2)], loc.at[0])
    own_b = pltpu.make_async_copy(mine_b, zb.at[pl.ds(2 * z, 2)], loc.at[1])
    own_a.start()
    own_b.start()

    own_s.wait()
    st_in = []
    for k, d in enumerate((1, n_req // 2)):
        taker = lax.rem(g + d, n_req)
        s0, s1 = slot_ref[2 * taker], slot_ref[2 * taker + 1]
        ssend[k] = sloc[lax.rem(jnp.where(s0 // 2 == g, s0, s1), 2)].astype(BF16)
    for k, d in enumerate((1, n_req // 2)):
        send(ssend.at[k], states.at[k], st_s.at[k], st_r.at[k], at_g(d))
        st_in.append((states.at[k], st_s.at[k], st_r.at[k], at_g(d)))

    wwait(0, wtmp.at[0], {"col": right})
    wsend(4, wtmp.at[0], w.at[left, first_h], {"col": right})
    tsend(2, tok_chunk(1), tok.at[c, chunk(1)], {"col": right})
    wwait(1, wtmp.at[1], {"col": left})
    wsend(5, wtmp.at[1], w.at[right, second_h], {"col": left})
    tsend(3, tok_chunk(0), tok.at[c, chunk(0)], {"col": left})

    for i, (frm, to) in enumerate(((left, right), (right, left))):
        wwait(2 + i, w.at[frm, mine_h], {"col": to})
        wsend(6 + 2 * i, w.at[frm, first_h], w.at[frm, first_h], at_x(1))
        wsend(7 + 2 * i, w.at[frm, second_h], w.at[frm, second_h], at_x(NX - 1))

    tile = 4 * BLK
    other = sib * half
    dev = {"row": sib}
    own_t.wait()
    own_w.wait()
    twait(4, tok.at[c, pl.ds(other, half)], dev)

    def share(q, fresh):
        def one(m, _):
            span = pl.ds(pl.multiple_of(m * tile, tile), tile)
            part_sum = jnp.dot(tok[q, span, :], w[q], preferred_element_type=F32)
            acc[span, :] = part_sum if fresh else acc[span, :] + part_sum
            return 0

        lax.fori_loop(0, NY, one, 0)

    share(c, True)

    slot_l0, slot_l1 = tok.at[left, chunk(0)], tok.at[left, chunk(1)]
    slot_r0, slot_r1 = tok.at[right, chunk(0)], tok.at[right, chunk(1)]
    slot_o0, slot_o1 = tok.at[opp, chunk(0)], tok.at[opp, chunk(1)]
    twait(0, slot_l0, {"col": right})
    tsend(5, slot_l0, slot_l0, {"col": right})
    tsend(6, slot_l0, slot_l0, {"row": sib})
    twait(1, slot_r1, {"col": left})
    tsend(7, slot_r1, slot_r1, {"col": left})
    tsend(8, slot_r1, slot_r1, {"row": sib})

    for got in z_in:
        landed(*got)
    own_a.wait()
    own_b.wait()
    for d in range(NX):
        gx = z * NX + lax.rem(x + d, NX)
        for j in range(2):
            p = row_ref[of_ref[j, gx]]
            idx = 2 * (p // (2 * NX)) + lax.rem(p, 2)
            if d == 0:
                xra[0, j] = za[idx]
                xrb[0, j] = zb[idx]
            else:
                xsa[d - 1, j] = za[idx]
                xsb[d - 1, j] = zb[idx]
    x_in = []
    for d in range(1, NX):
        for k, (src, dst) in enumerate(((xsa, xra), (xsb, xrb))):
            send(src.at[d - 1], dst.at[d], x_s.at[k, d], x_r.at[k, d], at_x(d))
            x_in.append((dst.at[d], x_s.at[k, d], x_r.at[k, d], at_x(d)))

    wwait(4, w.at[opp, first_h], {"col": right})
    wsend(10, w.at[opp, first_h], w.at[opp, first_h], at_x(1))
    wwait(5, w.at[opp, second_h], {"col": left})
    wsend(11, w.at[opp, second_h], w.at[opp, second_h], at_x(NX - 1))

    twait(2, slot_l1, {"col": right})
    tsend(9, slot_l1, slot_l1, {"row": sib})
    twait(3, slot_r0, {"col": left})
    tsend(10, slot_r0, slot_r0, {"row": sib})

    for got in x_in:
        landed(*got)
    for j in range(2):
        p = row_ref[of_ref[j, g]]
        xo = lax.rem(p // 2, NX)
        dd = lax.rem(x - xo + NX, NX)
        afull[pl.ds(16 * j, 16), pl.ds(fa, 128)] = xra[dd, j]
        bfull[j, pl.ds(4 * c, 4)] = xrb[dd, j]
    g_in = []
    ga = afull.at[:, pl.ds(fa, 128)]
    gb = bfull.at[:, pl.ds(4 * c, 4)]
    for i, (dr, dc) in enumerate(group):
        to = in_group(dr, dc)
        fc = lax.rem(c + NY - dc, NY)
        rf = 2 * fc + lax.rem(r + dr, 2)
        send(ga, ga, g_s.at[0, i], g_r.at[0, i], to)
        g_in.append((afull.at[:, pl.ds(pl.multiple_of(rf * 128, 128), 128)], g_s.at[0, i], g_r.at[0, i], to))
        if dr == 0:
            send(gb, gb, g_s.at[1, i], g_r.at[1, i], to)
            g_in.append((bfull.at[:, pl.ds(4 * fc, 4)], g_s.at[1, i], g_r.at[1, i], to))

    for i, (frm, to) in enumerate(((left, right), (right, left))):
        wwait(6 + 2 * i, w.at[frm, first_o], at_x(1))
        wwait(7 + 2 * i, w.at[frm, second_o], at_x(NX - 1))
    twait(6, tok.at[left, pl.ds(other, part)], dev)
    twait(9, tok.at[left, pl.ds(other + part, part)], dev)
    share(left, False)
    twait(10, tok.at[right, pl.ds(other, part)], dev)
    twait(8, tok.at[right, pl.ds(other + part, part)], dev)
    share(right, False)

    twait(5, slot_o0, {"col": right})
    tsend(11, slot_o0, slot_o0, {"row": sib})
    twait(7, slot_o1, {"col": left})
    tsend(12, slot_o1, slot_o1, {"row": sib})

    own_d.wait()
    for got in d_in + st_in + g_in:
        landed(*got)
    wwait(10, w.at[opp, first_o], at_x(1))
    wwait(11, w.at[opp, second_o], at_x(NX - 1))

    head_rows = lax.broadcasted_iota(jnp.int32, (4, 256), 0) == c
    for j in range(2):
        for k in range(16):
            row = jnp.sum(jnp.where(head_rows, bfull[j, k].astype(F32), 0.0), axis=0, keepdims=True)
            bh[pl.ds(16 * j + k, 1), :] = row

    first = len_ref[0, g]
    for j in range(2):
        s = slot_ref[2 * g + j]
        carry[j] = states[jnp.where(s // 2 == lax.rem(g + n_req - 1, n_req), 0, 1)].astype(F32)

    rows_i = lax.broadcasted_iota(jnp.int32, (tile, 1), 0)
    ti = lax.broadcasted_iota(jnp.int32, (tile, tile), 0)
    si = lax.broadcasted_iota(jnp.int32, (tile, tile), 1)
    seen = (ti // BLK == si // BLK) & (si <= ti)
    nt = (((1,), (1,)), ((), ()))
    tn = (((0,), (0,)), ((), ()))
    inv = 1.0 / math.sqrt(128.0)

    def one_tile(m, _):
        span = pl.ds(pl.multiple_of(m * tile, tile), tile)
        proj = acc[span, :] + jnp.dot(tok[opp, span, :], w[opp], preferred_element_type=F32)
        low = jnp.zeros((tile, 32), F32)
        for cc in range(NY):
            t = tok[cc, span, :]
            low += lax.dot_general(t, afull[:, cc * 256 : (cc + 1) * 256], nt, preferred_element_type=F32)
        request = (m * 4 + rows_i // BLK >= first).astype(jnp.int32)
        owner = lax.broadcasted_iota(jnp.int32, (tile, 32), 1) // 16
        low = jnp.where(owner == request, low, 0.0)
        hi = low.astype(BF16)
        lo = (low - hi.astype(F32)).astype(BF16)
        up = bh[...].astype(BF16)
        delta = jnp.dot(hi, up, preferred_element_type=F32) + jnp.dot(lo, up, preferred_element_type=F32)
        q = (proj[:, 0:128] + delta[:, 0:128]).astype(BF16)
        k = proj[:, 128:256].astype(BF16)
        v = (proj[:, 256:384] + delta[:, 128:256]).astype(BF16)
        gate = proj[:, 384:512].astype(BF16).astype(F32)
        qf, kf = q.astype(F32), k.astype(F32)
        sq = lax.rsqrt(jnp.mean(qf * qf, axis=1, keepdims=True) + 1e-06) * inv
        sk = lax.rsqrt(jnp.mean(kf * kf, axis=1, keepdims=True) + 1e-06) * inv
        vk = (v.astype(F32) * sk).astype(BF16)
        scores = lax.dot_general(q, k, nt, preferred_element_type=F32)
        scores = jnp.where(seen, scores, 0.0).astype(BF16)
        inner = jnp.dot(scores, vk, preferred_element_type=F32)
        dm = dec[m]
        fade = jnp.sum(
            jnp.where(lax.broadcasted_iota(jnp.int32, (4, 4), 1) == c, dm, 0.0), axis=1, keepdims=True
        )
        reads = []
        state = carry[0]
        for i in range(4):
            state = jnp.where(m * 4 + i == first, carry[1], state)
            sl = slice(i * BLK, (i + 1) * BLK)
            reads.append(jnp.dot(q[sl], state.astype(BF16), preferred_element_type=F32))
            upd = lax.dot_general(k[sl], vk[sl], tn, preferred_element_type=F32)
            state = state * fade[i : i + 1, :] + upd * (1.0 / BLK)
        carry[0] = state
        mem = (jnp.concatenate(reads, axis=0) + inner) * sq
        osend[m] = (mem * jax.nn.sigmoid(gate)).astype(BF16)

        place = out_ref.at[:, pl.ds(pl.multiple_of(c * 128, 128), 128)]

        @pl.when(m == c)
        def _():
            pltpu.make_async_copy(osend.at[m], place, loc.at[5]).start()

        @pl.when(m != c)
        def _():
            rem_copy(osend.at[m], place, o_s.at[m], o_r.at[c], {"col": m}).start()

        return 0

    twait(11, tok.at[opp, pl.ds(other, part)], dev)
    twait(12, tok.at[opp, pl.ds(other + part, part)], dev)
    lax.fori_loop(0, NY, one_tile, 0)

    for cp in sends:
        cp.wait_send()
    for d in range(1, NY):
        frm = lax.rem(c + d, NY)
        place = out_ref.at[:, pl.ds(pl.multiple_of(frm * 128, 128), 128)]
        cp = rem_copy(osend.at[frm], place, o_s.at[frm], o_r.at[frm], {"col": frm})
        cp.wait_send()
        cp.wait_recv()
    place = out_ref.at[:, pl.ds(pl.multiple_of(c * 128, 128), 128)]
    pltpu.make_async_copy(osend.at[c], place, loc.at[5]).wait()


def body(
    n_req, tokens, w_proj, adapter_a, adapter_b, adapter_row, adapter_of, len_blocks, state_slot, init_state, decay
):
    w_heads = jnp.transpose(w_proj, (1, 0, 2))
    a_t = jnp.swapaxes(adapter_a, 1, 2)
    nz = n_req // NX
    dma = pltpu.SemaphoreType.DMA
    smem = pl.BlockSpec(memory_space=pltpu.SMEM)
    anym = pl.BlockSpec(memory_space=pl.ANY)
    return pl.pallas_call(
        functools.partial(kernel, n_req),
        out_shape=jax.ShapeDtypeStruct((256, 512), BF16),
        in_specs=[smem] * 4 + [anym] * 5 + [pl.BlockSpec(memory_space=pltpu.VMEM)],
        out_specs=anym,
        scratch_shapes=[
            pltpu.VMEM((NY, 1024, 256), BF16),
            pltpu.VMEM((NY, 256, 512), BF16),
            pltpu.VMEM((2 * nz, 16, 128), BF16),
            pltpu.VMEM((2 * nz, 4, 4, 256), BF16),
            pltpu.VMEM((NX - 1, 2, 16, 128), BF16),
            pltpu.VMEM((NX - 1, 2, 4, 4, 256), BF16),
            pltpu.VMEM((NX, 2, 16, 128), BF16),
            pltpu.VMEM((NX, 2, 4, 4, 256), BF16),
            pltpu.VMEM((32, 1024), BF16),
            pltpu.VMEM((2, 16, 4, 256), BF16),
            pltpu.VMEM((32, 256), F32),
            pltpu.VMEM((2, 64, 512), BF16),
            pltpu.VMEM((1024, 512), F32),
            pltpu.VMEM((2, 128, 128), F32),
            pltpu.VMEM((2, 128, 128), BF16),
            pltpu.VMEM((2, 128, 128), BF16),
            pltpu.VMEM((NY, 4, 4), F32),
            pltpu.VMEM((2, 128, 128), F32),
            pltpu.VMEM((NY, 256, 128), BF16),
            dma((13,)),
            dma((13,)),
            dma((12,)),
            dma((12,)),
            dma((2, nz)),
            dma((2, nz)),
            dma((2, NX)),
            dma((2, NX)),
            dma((2, 7)),
            dma((2, 7)),
            dma((2,)),
            dma((2,)),
            dma((NY,)),
            dma((NY,)),
            dma((NY,)),
            dma((NY,)),
            dma((7,)),
            pltpu.SemaphoreType.REGULAR,
            pltpu.SemaphoreType.REGULAR,
            pltpu.SemaphoreType.REGULAR,
        ],
        compiler_params=pltpu.CompilerParams(collective_id=0, has_side_effects=True),
        name="memory_layer",
    )(
        adapter_row,
        jnp.transpose(adapter_of),
        jnp.transpose(len_blocks),
        state_slot,
        tokens,
        w_heads,
        a_t,
        adapter_b,
        init_state,
        decay,
    )


def solution(mesh):
    placed = (
        P(("req", "row"), "col"),
        P("col", "row", None),
        P("req", None, None),
        P("req", None, "row", None),
        P(),
        P(),
        P(),
        P(),
        P("req", "row", None, None),
        P(("req", "col"), "row"),
    )
    return jax.shard_map(
        functools.partial(body, mesh.shape["req"]),
        mesh=mesh,
        in_specs=placed,
        out_specs=P(("req", "col"), "row"),
        check_vma=False,
    )
```

```python
import functools
import math

import jax
import jax.numpy as jnp
from jax import lax
from jax.experimental import pallas as pl
from jax.experimental.pallas import tpu as pltpu
from jax.sharding import PartitionSpec as P

BLK = 64
NX = 4
NY = 4
MESH = pl.DeviceIdType.MESH
F32 = jnp.float32
BF16 = jnp.bfloat16


def kernel(
    n_req,
    row_ref,
    of_ref,
    len_ref,
    slot_ref,
    tok_ref,
    w_ref,
    a_ref,
    b_ref,
    state_ref,
    decay_ref,
    out_ref,
    tok,
    w,
    za,
    zb,
    xsa,
    xsb,
    xra,
    xrb,
    afull,
    bfull,
    bh,
    wtmp,
    acc,
    lowacc,
    sloc,
    ssend,
    states,
    dec,
    carry,
    osend,
    tok_s,
    tok_r,
    w_s,
    w_r,
    z_s,
    z_r,
    x_s,
    x_r,
    g_s,
    g_r,
    st_s,
    st_r,
    d_s,
    d_r,
    o_s,
    o_r,
    loc,
    up_sem,
    down_sem,
    side_sem,
):
    nz = n_req // NX
    g = lax.axis_index("req")
    r = lax.axis_index("row")
    c = lax.axis_index("col")
    z, x = g // NX, lax.rem(g, NX)
    sib = 1 - r
    right, left, opp = lax.rem(c + 1, NY), lax.rem(c + 3, NY), lax.rem(c + 2, NY)
    half = tok_ref.shape[0]
    part = half // 2
    base = r * half

    def rem_copy(src, dst, ssem, rsem, dev):
        return pltpu.make_async_remote_copy(
            src_ref=src, dst_ref=dst, send_sem=ssem, recv_sem=rsem, device_id=dev, device_id_type=MESH
        )

    def at_z(d):
        return {"req": lax.rem(z + d, nz) * NX + x}

    def at_x(d):
        return {"req": z * NX + lax.rem(x + d, NX)}

    def at_g(d):
        return {"req": lax.rem(g + d, n_req)}

    group = [(dr, dc) for dr in range(2) for dc in range(NY) if dr or dc]

    def in_group(dr, dc):
        return {"row": lax.rem(r + dr, 2), "col": lax.rem(c + dc, NY)}

    near = [in_group(*p) for p in group] + [at_z(1), at_z(nz - 1), at_x(1), at_x(NX - 1)]
    barrier = pltpu.get_barrier_semaphore()
    for dev in near:
        pl.semaphore_signal(barrier, inc=1, device_id=dev, device_id_type=MESH)
    pl.semaphore_wait(barrier, len(near))

    sends = []

    def send(src, dst, ssem, rsem, dev):
        cp = rem_copy(src, dst, ssem, rsem, dev)
        cp.start()
        sends.append(cp)

    def landed(slot, ssem, rsem, dev):
        rem_copy(slot, slot, ssem, rsem, dev).wait_recv()

    hrow = lax.rem(x, 2) * 128
    orow = 128 - hrow
    eighth = 64

    def wsend(i, src, dst, dev):
        send(src, dst, w_s.at[i], w_r.at[i], dev)

    def wwait(i, slot, dev):
        landed(slot, w_s.at[i], w_r.at[i], dev)

    mine_h = pl.ds(hrow, 128)
    first_h, second_h = pl.ds(hrow, eighth), pl.ds(hrow + eighth, eighth)
    first_o, second_o = pl.ds(orow, eighth), pl.ds(orow + eighth, eighth)
    wsend(0, w_ref.at[opp, first_h], wtmp.at[0], {"col": right})
    wsend(1, w_ref.at[opp, second_h], wtmp.at[1], {"col": left})
    wsend(2, w_ref.at[right, mine_h], w.at[c, mine_h], {"col": right})
    wsend(3, w_ref.at[left, mine_h], w.at[c, mine_h], {"col": left})

    def chunk(k):
        return pl.ds(base + k * part, part)

    def tsend(i, src, dst, dev):
        send(src, dst, tok_s.at[i], tok_r.at[i], dev)

    def twait(i, slot, dev):
        landed(slot, tok_s.at[i], tok_r.at[i], dev)

    def tok_chunk(k):
        return tok_ref.at[pl.ds(k * part, part)]

    tsend(0, tok_chunk(0), tok.at[c, chunk(0)], {"col": right})
    tsend(1, tok_chunk(1), tok.at[c, chunk(1)], {"col": left})
    tsend(4, tok_ref, tok.at[c, pl.ds(base, half)], {"row": sib})
    own_t = pltpu.make_async_copy(tok_ref, tok.at[c, pl.ds(base, half)], loc.at[3])
    own_t.start()
    own_w = pltpu.make_async_copy(w_ref.at[c], w.at[c], loc.at[2])
    own_w.start()
    own_s = pltpu.make_async_copy(state_ref.at[:, c], sloc, loc.at[6])
    own_s.start()

    d_in = []
    for d in range(1, NY):
        to, frm = lax.rem(c + d, NY), lax.rem(c + NY - d, NY)
        send(decay_ref, dec.at[c], d_s.at[d], d_r.at[d], {"col": to})
        d_in.append((dec.at[frm], d_s.at[d], d_r.at[d], {"col": to}))
    own_d = pltpu.make_async_copy(decay_ref, dec.at[c], loc.at[4])
    own_d.start()

    for step in range(3):
        pl.semaphore_signal(up_sem, inc=1, device_id=at_z(nz - 1), device_id_type=MESH)
        pl.semaphore_signal(down_sem, inc=1, device_id=at_z(1), device_id_type=MESH)
        if step == 0:
            pl.semaphore_signal(side_sem, inc=1, device_id=at_x(NX - 1), device_id_type=MESH)
            pl.semaphore_wait(side_sem, 1)
        pl.semaphore_wait(up_sem, 1)
        pl.semaphore_wait(down_sem, 1)

    f = 2 * c + r
    fa = pl.multiple_of(f * 128, 128)
    mine_a = a_ref.at[:, :, pl.ds(fa, 128)]
    mine_b = b_ref.at[:, pl.ds(4 * c, 4)]
    z_in = []
    for d in (4, 3, 5, 2, 6, 1, 7):
        zo = lax.rem(z + nz - d, nz)
        for k, (src, dst) in enumerate(((mine_a, za), (mine_b, zb))):
            send(src, dst.at[pl.ds(2 * z, 2)], z_s.at[k, d], z_r.at[k, d], at_z(d))
            z_in.append((dst.at[pl.ds(2 * zo, 2)], z_s.at[k, d], z_r.at[k, d], at_z(d)))
    own_a = pltpu.make_async_copy(mine_a, za.at[pl.ds(2 * z, 2)], loc.at[0])
    own_b = pltpu.make_async_copy(mine_b, zb.at[pl.ds(2 * z, 2)], loc.at[1])
    own_a.start()
    own_b.start()

    own_s.wait()
    st_in = []
    for k, d in enumerate((1, n_req // 2)):
        taker = lax.rem(g + d, n_req)
        s0, s1 = slot_ref[2 * taker], slot_ref[2 * taker + 1]
        ssend[k] = sloc[lax.rem(jnp.where(s0 // 2 == g, s0, s1), 2)].astype(BF16)
    for k, d in enumerate((1, n_req // 2)):
        send(ssend.at[k], states.at[k], st_s.at[k], st_r.at[k], at_g(d))
        st_in.append((states.at[k], st_s.at[k], st_r.at[k], at_g(d)))

    wwait(0, wtmp.at[0], {"col": right})
    wsend(4, wtmp.at[0], w.at[left, first_h], {"col": right})
    tsend(2, tok_chunk(1), tok.at[c, chunk(1)], {"col": right})
    wwait(1, wtmp.at[1], {"col": left})
    wsend(5, wtmp.at[1], w.at[right, second_h], {"col": left})
    tsend(3, tok_chunk(0), tok.at[c, chunk(0)], {"col": left})

    for i, (frm, to) in enumerate(((left, right), (right, left))):
        wwait(2 + i, w.at[frm, mine_h], {"col": to})
        wsend(6 + 2 * i, w.at[frm, first_h], w.at[frm, first_h], at_x(1))
        wsend(7 + 2 * i, w.at[frm, second_h], w.at[frm, second_h], at_x(NX - 1))

    tile = 4 * BLK
    other = sib * half
    dev = {"row": sib}
    own_t.wait()
    own_w.wait()
    twait(4, tok.at[c, pl.ds(other, half)], dev)

    def share(q, fresh):
        def one(m, _):
            span = pl.ds(pl.multiple_of(m * tile, tile), tile)
            part_sum = jnp.dot(tok[q, span, :], w[q], preferred_element_type=F32)
            acc[span, :] = part_sum if fresh else acc[span, :] + part_sum
            return 0

        lax.fori_loop(0, NY, one, 0)

    share(c, True)

    slot_l0, slot_l1 = tok.at[left, chunk(0)], tok.at[left, chunk(1)]
    slot_r0, slot_r1 = tok.at[right, chunk(0)], tok.at[right, chunk(1)]
    slot_o0, slot_o1 = tok.at[opp, chunk(0)], tok.at[opp, chunk(1)]
    twait(0, slot_l0, {"col": right})
    tsend(5, slot_l0, slot_l0, {"col": right})
    tsend(6, slot_l0, slot_l0, {"row": sib})
    twait(1, slot_r1, {"col": left})
    tsend(7, slot_r1, slot_r1, {"col": left})
    tsend(8, slot_r1, slot_r1, {"row": sib})

    for got in z_in:
        landed(*got)
    own_a.wait()
    own_b.wait()
    for d in range(NX):
        gx = z * NX + lax.rem(x + d, NX)
        for j in range(2):
            p = row_ref[of_ref[j, gx]]
            idx = 2 * (p // (2 * NX)) + lax.rem(p, 2)
            if d == 0:
                xra[0, j] = za[idx]
                xrb[0, j] = zb[idx]
            else:
                xsa[d - 1, j] = za[idx]
                xsb[d - 1, j] = zb[idx]
    x_in = []
    for d in range(1, NX):
        for k, (src, dst) in enumerate(((xsa, xra), (xsb, xrb))):
            send(src.at[d - 1], dst.at[d], x_s.at[k, d], x_r.at[k, d], at_x(d))
            x_in.append((dst.at[d], x_s.at[k, d], x_r.at[k, d], at_x(d)))

    wwait(4, w.at[opp, first_h], {"col": right})
    wsend(10, w.at[opp, first_h], w.at[opp, first_h], at_x(1))
    wwait(5, w.at[opp, second_h], {"col": left})
    wsend(11, w.at[opp, second_h], w.at[opp, second_h], at_x(NX - 1))

    twait(2, slot_l1, {"col": right})
    tsend(9, slot_l1, slot_l1, {"row": sib})
    twait(3, slot_r0, {"col": left})
    tsend(10, slot_r0, slot_r0, {"row": sib})

    for got in x_in:
        landed(*got)
    for j in range(2):
        p = row_ref[of_ref[j, g]]
        xo = lax.rem(p // 2, NX)
        dd = lax.rem(x - xo + NX, NX)
        afull[pl.ds(16 * j, 16), pl.ds(fa, 128)] = xra[dd, j]
        bfull[j, pl.ds(4 * c, 4)] = xrb[dd, j]
    g_in = []
    ga = afull.at[:, pl.ds(fa, 128)]
    gb = bfull.at[:, pl.ds(4 * c, 4)]
    for i, (dr, dc) in enumerate(group):
        to = in_group(dr, dc)
        fc = lax.rem(c + NY - dc, NY)
        rf = 2 * fc + lax.rem(r + dr, 2)
        send(ga, ga, g_s.at[0, i], g_r.at[0, i], to)
        g_in.append((afull.at[:, pl.ds(pl.multiple_of(rf * 128, 128), 128)], g_s.at[0, i], g_r.at[0, i], to))
        if dr == 0:
            send(gb, gb, g_s.at[1, i], g_r.at[1, i], to)
            g_in.append((bfull.at[:, pl.ds(4 * fc, 4)], g_s.at[1, i], g_r.at[1, i], to))

    for i, (frm, to) in enumerate(((left, right), (right, left))):
        wwait(6 + 2 * i, w.at[frm, first_o], at_x(1))
        wwait(7 + 2 * i, w.at[frm, second_o], at_x(NX - 1))
    twait(6, tok.at[left, pl.ds(other, part)], dev)
    twait(9, tok.at[left, pl.ds(other + part, part)], dev)
    share(left, False)
    twait(10, tok.at[right, pl.ds(other, part)], dev)
    twait(8, tok.at[right, pl.ds(other + part, part)], dev)
    share(right, False)

    twait(5, slot_o0, {"col": right})
    tsend(11, slot_o0, slot_o0, {"row": sib})
    twait(7, slot_o1, {"col": left})
    tsend(12, slot_o1, slot_o1, {"row": sib})

    own_d.wait()
    for got in d_in + st_in + g_in:
        landed(*got)
    wwait(10, w.at[opp, first_o], at_x(1))
    wwait(11, w.at[opp, second_o], at_x(NX - 1))

    head_rows = lax.broadcasted_iota(jnp.int32, (4, 256), 0) == c
    for j in range(2):
        for k in range(16):
            row = jnp.sum(jnp.where(head_rows, bfull[j, k].astype(F32), 0.0), axis=0, keepdims=True)
            bh[pl.ds(16 * j + k, 1), :] = row

    first = len_ref[0, g]
    for j in range(2):
        s = slot_ref[2 * g + j]
        carry[j] = states[jnp.where(s // 2 == lax.rem(g + n_req - 1, n_req), 0, 1)].astype(F32)

    rows_i = lax.broadcasted_iota(jnp.int32, (tile, 1), 0)
    ti = lax.broadcasted_iota(jnp.int32, (tile, tile), 0)
    si = lax.broadcasted_iota(jnp.int32, (tile, tile), 1)
    seen = (ti // BLK == si // BLK) & (si <= ti)
    nt = (((1,), (1,)), ((), ()))
    tn = (((0,), (0,)), ((), ()))
    inv = 1.0 / math.sqrt(128.0)

    def low_share(q, span):
        maps = afull[:, pl.ds(pl.multiple_of(q * 256, 256), 256)]
        return lax.dot_general(tok[q, span, :], maps, nt, preferred_element_type=F32)

    def low_three(m, _):
        span = pl.ds(pl.multiple_of(m * tile, tile), tile)
        lowacc[span, :] = low_share(c, span) + low_share(left, span) + low_share(right, span)
        return 0

    def last_share(m):
        span = pl.ds(pl.multiple_of(m * tile, tile), tile)
        acc[span, :] += jnp.dot(tok[opp, span, :], w[opp], preferred_element_type=F32)
        lowacc[span, :] += low_share(opp, span)

    lax.fori_loop(0, NY, low_three, 0)

    def own_share(m, _):
        last_share(2 * r + m)
        return 0

    lax.fori_loop(0, 2, own_share, 0)

    def one_tile(m, _):
        @pl.when(m // 2 != r)
        def _():
            twait(11 + lax.rem(m, 2), tok.at[opp, pl.ds(pl.multiple_of(m * tile, tile), tile)], dev)
            last_share(m)

        span = pl.ds(pl.multiple_of(m * tile, tile), tile)
        proj = acc[span, :]
        low = lowacc[span, :]
        request = (m * 4 + rows_i // BLK >= first).astype(jnp.int32)
        owner = lax.broadcasted_iota(jnp.int32, (tile, 32), 1) // 16
        low = jnp.where(owner == request, low, 0.0)
        hi = low.astype(BF16)
        lo = (low - hi.astype(F32)).astype(BF16)
        up = bh[...].astype(BF16)
        delta = jnp.dot(hi, up, preferred_element_type=F32) + jnp.dot(lo, up, preferred_element_type=F32)
        q = (proj[:, 0:128] + delta[:, 0:128]).astype(BF16)
        k = proj[:, 128:256].astype(BF16)
        v = (proj[:, 256:384] + delta[:, 128:256]).astype(BF16)
        gate = proj[:, 384:512].astype(BF16).astype(F32)
        qf, kf = q.astype(F32), k.astype(F32)
        sq = lax.rsqrt(jnp.mean(qf * qf, axis=1, keepdims=True) + 1e-06) * inv
        sk = lax.rsqrt(jnp.mean(kf * kf, axis=1, keepdims=True) + 1e-06) * inv
        vk = (v.astype(F32) * sk).astype(BF16)
        scores = lax.dot_general(q, k, nt, preferred_element_type=F32)
        scores = jnp.where(seen, scores, 0.0).astype(BF16)
        inner = jnp.dot(scores, vk, preferred_element_type=F32)
        dm = dec[m]
        fade = jnp.sum(
            jnp.where(lax.broadcasted_iota(jnp.int32, (4, 4), 1) == c, dm, 0.0), axis=1, keepdims=True
        )
        reads = []
        state = carry[0]
        for i in range(4):
            state = jnp.where(m * 4 + i == first, carry[1], state)
            sl = slice(i * BLK, (i + 1) * BLK)
            reads.append(jnp.dot(q[sl], state.astype(BF16), preferred_element_type=F32))
            upd = lax.dot_general(k[sl], vk[sl], tn, preferred_element_type=F32)
            state = state * fade[i : i + 1, :] + upd * (1.0 / BLK)
        carry[0] = state
        mem = (jnp.concatenate(reads, axis=0) + inner) * sq
        osend[m] = (mem * jax.nn.sigmoid(gate)).astype(BF16)

        place = out_ref.at[:, pl.ds(pl.multiple_of(c * 128, 128), 128)]

        @pl.when(m == c)
        def _():
            pltpu.make_async_copy(osend.at[m], place, loc.at[5]).start()

        @pl.when(m != c)
        def _():
            rem_copy(osend.at[m], place, o_s.at[m], o_r.at[c], {"col": m}).start()

        return 0

    lax.fori_loop(0, NY, one_tile, 0)

    for cp in sends:
        cp.wait_send()
    for d in range(1, NY):
        frm = lax.rem(c + d, NY)
        place = out_ref.at[:, pl.ds(pl.multiple_of(frm * 128, 128), 128)]
        cp = rem_copy(osend.at[frm], place, o_s.at[frm], o_r.at[frm], {"col": frm})
        cp.wait_send()
        cp.wait_recv()
    place = out_ref.at[:, pl.ds(pl.multiple_of(c * 128, 128), 128)]
    pltpu.make_async_copy(osend.at[c], place, loc.at[5]).wait()


def body(
    n_req, tokens, w_proj, adapter_a, adapter_b, adapter_row, adapter_of, len_blocks, state_slot, init_state, decay
):
    w_heads = jnp.transpose(w_proj, (1, 0, 2))
    a_t = jnp.swapaxes(adapter_a, 1, 2)
    nz = n_req // NX
    dma = pltpu.SemaphoreType.DMA
    smem = pl.BlockSpec(memory_space=pltpu.SMEM)
    anym = pl.BlockSpec(memory_space=pl.ANY)
    return pl.pallas_call(
        functools.partial(kernel, n_req),
        out_shape=jax.ShapeDtypeStruct((256, 512), BF16),
        in_specs=[smem] * 4 + [anym] * 5 + [pl.BlockSpec(memory_space=pltpu.VMEM)],
        out_specs=anym,
        scratch_shapes=[
            pltpu.VMEM((NY, 1024, 256), BF16),
            pltpu.VMEM((NY, 256, 512), BF16),
            pltpu.VMEM((2 * nz, 16, 128), BF16),
            pltpu.VMEM((2 * nz, 4, 4, 256), BF16),
            pltpu.VMEM((NX - 1, 2, 16, 128), BF16),
            pltpu.VMEM((NX - 1, 2, 4, 4, 256), BF16),
            pltpu.VMEM((NX, 2, 16, 128), BF16),
            pltpu.VMEM((NX, 2, 4, 4, 256), BF16),
            pltpu.VMEM((32, 1024), BF16),
            pltpu.VMEM((2, 16, 4, 256), BF16),
            pltpu.VMEM((32, 256), F32),
            pltpu.VMEM((2, 64, 512), BF16),
            pltpu.VMEM((1024, 512), F32),
            pltpu.VMEM((1024, 32), F32),
            pltpu.VMEM((2, 128, 128), F32),
            pltpu.VMEM((2, 128, 128), BF16),
            pltpu.VMEM((2, 128, 128), BF16),
            pltpu.VMEM((NY, 4, 4), F32),
            pltpu.VMEM((2, 128, 128), F32),
            pltpu.VMEM((NY, 256, 128), BF16),
            dma((13,)),
            dma((13,)),
            dma((12,)),
            dma((12,)),
            dma((2, nz)),
            dma((2, nz)),
            dma((2, NX)),
            dma((2, NX)),
            dma((2, 7)),
            dma((2, 7)),
            dma((2,)),
            dma((2,)),
            dma((NY,)),
            dma((NY,)),
            dma((NY,)),
            dma((NY,)),
            dma((7,)),
            pltpu.SemaphoreType.REGULAR,
            pltpu.SemaphoreType.REGULAR,
            pltpu.SemaphoreType.REGULAR,
        ],
        compiler_params=pltpu.CompilerParams(collective_id=0, has_side_effects=True),
        name="memory_layer",
    )(
        adapter_row,
        jnp.transpose(adapter_of),
        jnp.transpose(len_blocks),
        state_slot,
        tokens,
        w_heads,
        a_t,
        adapter_b,
        init_state,
        decay,
    )


def solution(mesh):
    placed = (
        P(("req", "row"), "col"),
        P("col", "row", None),
        P("req", None, None),
        P("req", None, "row", None),
        P(),
        P(),
        P(),
        P(),
        P("req", "row", None, None),
        P(("req", "col"), "row"),
    )
    return jax.shard_map(
        functools.partial(body, mesh.shape["req"]),
        mesh=mesh,
        in_specs=placed,
        out_specs=P(("req", "col"), "row"),
        check_vma=False,
    )
```

```python
import functools
import math

import jax
import jax.numpy as jnp
from jax import lax
from jax.experimental import pallas as pl
from jax.experimental.pallas import tpu as pltpu
from jax.sharding import PartitionSpec as P

BLK = 64
NX = 4
NY = 4
MESH = pl.DeviceIdType.MESH
F32 = jnp.float32
BF16 = jnp.bfloat16


def kernel(
    n_req,
    row_ref,
    of_ref,
    len_ref,
    slot_ref,
    tok_ref,
    w_ref,
    a_ref,
    b_ref,
    state_ref,
    decay_ref,
    out_ref,
    tok,
    w,
    za,
    zb,
    xsa,
    xsb,
    xra,
    xrb,
    afull,
    bfull,
    bh,
    wtmp,
    wraw,
    wl,
    acc,
    sloc,
    ssend,
    states,
    dec,
    carry,
    osend,
    tok_s,
    tok_r,
    w_s,
    w_r,
    z_s,
    z_r,
    x_s,
    x_r,
    g_s,
    g_r,
    st_s,
    st_r,
    d_s,
    d_r,
    o_s,
    o_r,
    loc,
    up_sem,
    down_sem,
    side_sem,
):
    nz = n_req // NX
    g = lax.axis_index("req")
    r = lax.axis_index("row")
    c = lax.axis_index("col")
    z, x = g // NX, lax.rem(g, NX)
    sib = 1 - r
    right, left, opp = lax.rem(c + 1, NY), lax.rem(c + 3, NY), lax.rem(c + 2, NY)
    half = tok_ref.shape[0]
    part = half // 2
    base = r * half

    def rem_copy(src, dst, ssem, rsem, dev):
        return pltpu.make_async_remote_copy(
            src_ref=src, dst_ref=dst, send_sem=ssem, recv_sem=rsem, device_id=dev, device_id_type=MESH
        )

    def at_z(d):
        return {"req": lax.rem(z + d, nz) * NX + x}

    def at_x(d):
        return {"req": z * NX + lax.rem(x + d, NX)}

    def at_g(d):
        return {"req": lax.rem(g + d, n_req)}

    group = [(dr, dc) for dr in range(2) for dc in range(NY) if dr or dc]

    def in_group(dr, dc):
        return {"row": lax.rem(r + dr, 2), "col": lax.rem(c + dc, NY)}

    raw = pltpu.make_async_copy(w_ref, wraw, loc.at[7])
    raw.start()

    near = [in_group(*p) for p in group] + [at_z(1), at_z(nz - 1), at_x(1), at_x(NX - 1)]
    barrier = pltpu.get_barrier_semaphore()
    for dev in near:
        pl.semaphore_signal(barrier, inc=1, device_id=dev, device_id_type=MESH)

    raw.wait()

    def regroup(i, _):
        span = pl.ds(pl.multiple_of(32 * i, 32), 32)
        for h in range(NY):
            wl[h, span, :] = wraw[span, h, :]
        return 0

    lax.fori_loop(0, 8, regroup, 0)
    pl.semaphore_wait(barrier, len(near))

    sends = []

    def send(src, dst, ssem, rsem, dev):
        cp = rem_copy(src, dst, ssem, rsem, dev)
        cp.start()
        sends.append(cp)

    def landed(slot, ssem, rsem, dev):
        rem_copy(slot, slot, ssem, rsem, dev).wait_recv()

    hrow = lax.rem(x, 2) * 128
    orow = 128 - hrow
    eighth = 64

    def wsend(i, src, dst, dev):
        send(src, dst, w_s.at[i], w_r.at[i], dev)

    def wwait(i, slot, dev):
        landed(slot, w_s.at[i], w_r.at[i], dev)

    mine_h = pl.ds(hrow, 128)
    first_h, second_h = pl.ds(hrow, eighth), pl.ds(hrow + eighth, eighth)
    first_o, second_o = pl.ds(orow, eighth), pl.ds(orow + eighth, eighth)
    wsend(0, wl.at[opp, first_h], wtmp.at[0], {"col": right})
    wsend(1, wl.at[opp, second_h], wtmp.at[1], {"col": left})
    wsend(2, wl.at[right, mine_h], w.at[c, mine_h], {"col": right})
    wsend(3, wl.at[left, mine_h], w.at[c, mine_h], {"col": left})

    def chunk(k):
        return pl.ds(base + k * part, part)

    def tsend(i, src, dst, dev):
        send(src, dst, tok_s.at[i], tok_r.at[i], dev)

    def twait(i, slot, dev):
        landed(slot, tok_s.at[i], tok_r.at[i], dev)

    def tok_chunk(k):
        return tok_ref.at[pl.ds(k * part, part)]

    tsend(0, tok_chunk(0), tok.at[c, chunk(0)], {"col": right})
    tsend(1, tok_chunk(1), tok.at[c, chunk(1)], {"col": left})
    tsend(4, tok_ref, tok.at[c, pl.ds(base, half)], {"row": sib})
    own_t = pltpu.make_async_copy(tok_ref, tok.at[c, pl.ds(base, half)], loc.at[3])
    own_t.start()
    own_w = pltpu.make_async_copy(wl.at[c], w.at[c], loc.at[2])
    own_w.start()
    own_s = pltpu.make_async_copy(state_ref.at[:, c], sloc, loc.at[6])
    own_s.start()

    d_in = []
    for d in range(1, NY):
        to, frm = lax.rem(c + d, NY), lax.rem(c + NY - d, NY)
        send(decay_ref, dec.at[c], d_s.at[d], d_r.at[d], {"col": to})
        d_in.append((dec.at[frm], d_s.at[d], d_r.at[d], {"col": to}))
    own_d = pltpu.make_async_copy(decay_ref, dec.at[c], loc.at[4])
    own_d.start()

    for step in range(3):
        pl.semaphore_signal(up_sem, inc=1, device_id=at_z(nz - 1), device_id_type=MESH)
        pl.semaphore_signal(down_sem, inc=1, device_id=at_z(1), device_id_type=MESH)
        if step == 0:
            pl.semaphore_signal(side_sem, inc=1, device_id=at_x(NX - 1), device_id_type=MESH)
            pl.semaphore_wait(side_sem, 1)
        pl.semaphore_wait(up_sem, 1)
        pl.semaphore_wait(down_sem, 1)

    f = 2 * c + r
    fa = pl.multiple_of(f * 128, 128)
    mine_a = a_ref.at[:, :, pl.ds(fa, 128)]
    mine_b = b_ref.at[:, pl.ds(4 * c, 4)]
    z_in = []
    for d in (4, 3, 5, 2, 6, 1, 7):
        zo = lax.rem(z + nz - d, nz)
        for k, (src, dst) in enumerate(((mine_a, za), (mine_b, zb))):
            send(src, dst.at[pl.ds(2 * z, 2)], z_s.at[k, d], z_r.at[k, d], at_z(d))
            z_in.append((dst.at[pl.ds(2 * zo, 2)], z_s.at[k, d], z_r.at[k, d], at_z(d)))
    own_a = pltpu.make_async_copy(mine_a, za.at[pl.ds(2 * z, 2)], loc.at[0])
    own_b = pltpu.make_async_copy(mine_b, zb.at[pl.ds(2 * z, 2)], loc.at[1])
    own_a.start()
    own_b.start()

    own_s.wait()
    st_in = []
    for k, d in enumerate((1, n_req // 2)):
        taker = lax.rem(g + d, n_req)
        s0, s1 = slot_ref[2 * taker], slot_ref[2 * taker + 1]
        ssend[k] = sloc[lax.rem(jnp.where(s0 // 2 == g, s0, s1), 2)].astype(BF16)
    for k, d in enumerate((1, n_req // 2)):
        send(ssend.at[k], states.at[k], st_s.at[k], st_r.at[k], at_g(d))
        st_in.append((states.at[k], st_s.at[k], st_r.at[k], at_g(d)))

    wwait(0, wtmp.at[0], {"col": right})
    wsend(4, wtmp.at[0], w.at[left, first_h], {"col": right})
    tsend(2, tok_chunk(1), tok.at[c, chunk(1)], {"col": right})
    wwait(1, wtmp.at[1], {"col": left})
    wsend(5, wtmp.at[1], w.at[right, second_h], {"col": left})
    tsend(3, tok_chunk(0), tok.at[c, chunk(0)], {"col": left})

    for i, (frm, to) in enumerate(((left, right), (right, left))):
        wwait(2 + i, w.at[frm, mine_h], {"col": to})
        wsend(6 + 2 * i, w.at[frm, first_h], w.at[frm, first_h], at_x(1))
        wsend(7 + 2 * i, w.at[frm, second_h], w.at[frm, second_h], at_x(NX - 1))

    tile = 4 * BLK
    other = sib * half
    dev = {"row": sib}
    own_t.wait()
    own_w.wait()
    twait(4, tok.at[c, pl.ds(other, half)], dev)

    def share(q, fresh):
        def one(m, _):
            span = pl.ds(pl.multiple_of(m * tile, tile), tile)
            part_sum = jnp.dot(tok[q, span, :], w[q], preferred_element_type=F32)
            acc[span, :] = part_sum if fresh else acc[span, :] + part_sum
            return 0

        lax.fori_loop(0, NY, one, 0)

    share(c, True)

    slot_l0, slot_l1 = tok.at[left, chunk(0)], tok.at[left, chunk(1)]
    slot_r0, slot_r1 = tok.at[right, chunk(0)], tok.at[right, chunk(1)]
    slot_o0, slot_o1 = tok.at[opp, chunk(0)], tok.at[opp, chunk(1)]
    twait(0, slot_l0, {"col": right})
    tsend(5, slot_l0, slot_l0, {"col": right})
    tsend(6, slot_l0, slot_l0, {"row": sib})
    twait(1, slot_r1, {"col": left})
    tsend(7, slot_r1, slot_r1, {"col": left})
    tsend(8, slot_r1, slot_r1, {"row": sib})

    for got in z_in:
        landed(*got)
    own_a.wait()
    own_b.wait()
    for d in range(NX):
        gx = z * NX + lax.rem(x + d, NX)
        for j in range(2):
            p = row_ref[of_ref[j, gx]]
            idx = 2 * (p // (2 * NX)) + lax.rem(p, 2)
            if d == 0:
                xra[0, j] = za[idx]
                xrb[0, j] = zb[idx]
            else:
                xsa[d - 1, j] = za[idx]
                xsb[d - 1, j] = zb[idx]
    x_in = []
    for d in range(1, NX):
        for k, (src, dst) in enumerate(((xsa, xra), (xsb, xrb))):
            send(src.at[d - 1], dst.at[d], x_s.at[k, d], x_r.at[k, d], at_x(d))
            x_in.append((dst.at[d], x_s.at[k, d], x_r.at[k, d], at_x(d)))

    wwait(4, w.at[opp, first_h], {"col": right})
    wsend(10, w.at[opp, first_h], w.at[opp, first_h], at_x(1))
    wwait(5, w.at[opp, second_h], {"col": left})
    wsend(11, w.at[opp, second_h], w.at[opp, second_h], at_x(NX - 1))

    twait(2, slot_l1, {"col": right})
    tsend(9, slot_l1, slot_l1, {"row": sib})
    twait(3, slot_r0, {"col": left})
    tsend(10, slot_r0, slot_r0, {"row": sib})

    for got in x_in:
        landed(*got)
    for j in range(2):
        p = row_ref[of_ref[j, g]]
        xo = lax.rem(p // 2, NX)
        dd = lax.rem(x - xo + NX, NX)
        afull[pl.ds(16 * j, 16), pl.ds(fa, 128)] = xra[dd, j]
        bfull[j, pl.ds(4 * c, 4)] = xrb[dd, j]
    g_in = []
    ga = afull.at[:, pl.ds(fa, 128)]
    gb = bfull.at[:, pl.ds(4 * c, 4)]
    for i, (dr, dc) in enumerate(group):
        to = in_group(dr, dc)
        fc = lax.rem(c + NY - dc, NY)
        rf = 2 * fc + lax.rem(r + dr, 2)
        send(ga, ga, g_s.at[0, i], g_r.at[0, i], to)
        g_in.append((afull.at[:, pl.ds(pl.multiple_of(rf * 128, 128), 128)], g_s.at[0, i], g_r.at[0, i], to))
        if dr == 0:
            send(gb, gb, g_s.at[1, i], g_r.at[1, i], to)
            g_in.append((bfull.at[:, pl.ds(4 * fc, 4)], g_s.at[1, i], g_r.at[1, i], to))

    for i, (frm, to) in enumerate(((left, right), (right, left))):
        wwait(6 + 2 * i, w.at[frm, first_o], at_x(1))
        wwait(7 + 2 * i, w.at[frm, second_o], at_x(NX - 1))
    twait(6, tok.at[left, pl.ds(other, part)], dev)
    twait(9, tok.at[left, pl.ds(other + part, part)], dev)
    share(left, False)
    twait(10, tok.at[right, pl.ds(other, part)], dev)
    twait(8, tok.at[right, pl.ds(other + part, part)], dev)
    share(right, False)

    twait(5, slot_o0, {"col": right})
    tsend(11, slot_o0, slot_o0, {"row": sib})
    twait(7, slot_o1, {"col": left})
    tsend(12, slot_o1, slot_o1, {"row": sib})

    own_d.wait()
    for got in d_in + st_in + g_in:
        landed(*got)
    wwait(10, w.at[opp, first_o], at_x(1))
    wwait(11, w.at[opp, second_o], at_x(NX - 1))

    head_rows = lax.broadcasted_iota(jnp.int32, (4, 256), 0) == c
    for j in range(2):
        for k in range(16):
            row = jnp.sum(jnp.where(head_rows, bfull[j, k].astype(F32), 0.0), axis=0, keepdims=True)
            bh[pl.ds(16 * j + k, 1), :] = row

    first = len_ref[0, g]
    for j in range(2):
        s = slot_ref[2 * g + j]
        carry[j] = states[jnp.where(s // 2 == lax.rem(g + n_req - 1, n_req), 0, 1)].astype(F32)

    rows_i = lax.broadcasted_iota(jnp.int32, (tile, 1), 0)
    ti = lax.broadcasted_iota(jnp.int32, (tile, tile), 0)
    si = lax.broadcasted_iota(jnp.int32, (tile, tile), 1)
    seen = (ti // BLK == si // BLK) & (si <= ti)
    nt = (((1,), (1,)), ((), ()))
    tn = (((0,), (0,)), ((), ()))
    inv = 1.0 / math.sqrt(128.0)

    def one_tile(m, _):
        span = pl.ds(pl.multiple_of(m * tile, tile), tile)
        proj = acc[span, :] + jnp.dot(tok[opp, span, :], w[opp], preferred_element_type=F32)
        low = jnp.zeros((tile, 32), F32)
        for cc in range(NY):
            t = tok[cc, span, :]
            low += lax.dot_general(t, afull[:, cc * 256 : (cc + 1) * 256], nt, preferred_element_type=F32)
        request = (m * 4 + rows_i // BLK >= first).astype(jnp.int32)
        owner = lax.broadcasted_iota(jnp.int32, (tile, 32), 1) // 16
        low = jnp.where(owner == request, low, 0.0)
        hi = low.astype(BF16)
        lo = (low - hi.astype(F32)).astype(BF16)
        up = bh[...].astype(BF16)
        delta = jnp.dot(hi, up, preferred_element_type=F32) + jnp.dot(lo, up, preferred_element_type=F32)
        q = (proj[:, 0:128] + delta[:, 0:128]).astype(BF16)
        k = proj[:, 128:256].astype(BF16)
        v = (proj[:, 256:384] + delta[:, 128:256]).astype(BF16)
        gate = proj[:, 384:512].astype(BF16).astype(F32)
        qf, kf = q.astype(F32), k.astype(F32)
        sq = lax.rsqrt(jnp.mean(qf * qf, axis=1, keepdims=True) + 1e-06) * inv
        sk = lax.rsqrt(jnp.mean(kf * kf, axis=1, keepdims=True) + 1e-06) * inv
        vk = (v.astype(F32) * sk).astype(BF16)
        scores = lax.dot_general(q, k, nt, preferred_element_type=F32)
        scores = jnp.where(seen, scores, 0.0).astype(BF16)
        inner = jnp.dot(scores, vk, preferred_element_type=F32)
        dm = dec[m]
        fade = jnp.sum(
            jnp.where(lax.broadcasted_iota(jnp.int32, (4, 4), 1) == c, dm, 0.0), axis=1, keepdims=True
        )
        reads = []
        state = carry[0]
        for i in range(4):
            state = jnp.where(m * 4 + i == first, carry[1], state)
            sl = slice(i * BLK, (i + 1) * BLK)
            reads.append(jnp.dot(q[sl], state.astype(BF16), preferred_element_type=F32))
            upd = lax.dot_general(k[sl], vk[sl], tn, preferred_element_type=F32)
            state = state * fade[i : i + 1, :] + upd * (1.0 / BLK)
        carry[0] = state
        mem = (jnp.concatenate(reads, axis=0) + inner) * sq
        osend[m] = (mem * jax.nn.sigmoid(gate)).astype(BF16)

        place = out_ref.at[:, pl.ds(pl.multiple_of(c * 128, 128), 128)]

        @pl.when(m == c)
        def _():
            pltpu.make_async_copy(osend.at[m], place, loc.at[5]).start()

        @pl.when(m != c)
        def _():
            rem_copy(osend.at[m], place, o_s.at[m], o_r.at[c], {"col": m}).start()

        return 0

    twait(11, tok.at[opp, pl.ds(other, part)], dev)
    twait(12, tok.at[opp, pl.ds(other + part, part)], dev)
    lax.fori_loop(0, NY, one_tile, 0)

    for cp in sends:
        cp.wait_send()
    for d in range(1, NY):
        frm = lax.rem(c + d, NY)
        place = out_ref.at[:, pl.ds(pl.multiple_of(frm * 128, 128), 128)]
        cp = rem_copy(osend.at[frm], place, o_s.at[frm], o_r.at[frm], {"col": frm})
        cp.wait_send()
        cp.wait_recv()
    place = out_ref.at[:, pl.ds(pl.multiple_of(c * 128, 128), 128)]
    pltpu.make_async_copy(osend.at[c], place, loc.at[5]).wait()


def body(
    n_req, tokens, w_proj, adapter_a, adapter_b, adapter_row, adapter_of, len_blocks, state_slot, init_state, decay
):
    a_t = jnp.swapaxes(adapter_a, 1, 2)
    nz = n_req // NX
    dma = pltpu.SemaphoreType.DMA
    smem = pl.BlockSpec(memory_space=pltpu.SMEM)
    anym = pl.BlockSpec(memory_space=pl.ANY)
    return pl.pallas_call(
        functools.partial(kernel, n_req),
        out_shape=jax.ShapeDtypeStruct((256, 512), BF16),
        in_specs=[smem] * 4 + [anym] * 5 + [pl.BlockSpec(memory_space=pltpu.VMEM)],
        out_specs=anym,
        scratch_shapes=[
            pltpu.VMEM((NY, 1024, 256), BF16),
            pltpu.VMEM((NY, 256, 512), BF16),
            pltpu.VMEM((2 * nz, 16, 128), BF16),
            pltpu.VMEM((2 * nz, 4, 4, 256), BF16),
            pltpu.VMEM((NX - 1, 2, 16, 128), BF16),
            pltpu.VMEM((NX - 1, 2, 4, 4, 256), BF16),
            pltpu.VMEM((NX, 2, 16, 128), BF16),
            pltpu.VMEM((NX, 2, 4, 4, 256), BF16),
            pltpu.VMEM((32, 1024), BF16),
            pltpu.VMEM((2, 16, 4, 256), BF16),
            pltpu.VMEM((32, 256), F32),
            pltpu.VMEM((2, 64, 512), BF16),
            pltpu.VMEM((256, NY, 512), BF16),
            pltpu.VMEM((NY, 256, 512), BF16),
            pltpu.VMEM((1024, 512), F32),
            pltpu.VMEM((2, 128, 128), F32),
            pltpu.VMEM((2, 128, 128), BF16),
            pltpu.VMEM((2, 128, 128), BF16),
            pltpu.VMEM((NY, 4, 4), F32),
            pltpu.VMEM((2, 128, 128), F32),
            pltpu.VMEM((NY, 256, 128), BF16),
            dma((13,)),
            dma((13,)),
            dma((12,)),
            dma((12,)),
            dma((2, nz)),
            dma((2, nz)),
            dma((2, NX)),
            dma((2, NX)),
            dma((2, 7)),
            dma((2, 7)),
            dma((2,)),
            dma((2,)),
            dma((NY,)),
            dma((NY,)),
            dma((NY,)),
            dma((NY,)),
            dma((8,)),
            pltpu.SemaphoreType.REGULAR,
            pltpu.SemaphoreType.REGULAR,
            pltpu.SemaphoreType.REGULAR,
        ],
        compiler_params=pltpu.CompilerParams(collective_id=0, has_side_effects=True),
        name="memory_layer",
    )(
        adapter_row,
        jnp.transpose(adapter_of),
        jnp.transpose(len_blocks),
        state_slot,
        tokens,
        w_proj,
        a_t,
        adapter_b,
        init_state,
        decay,
    )


def solution(mesh):
    placed = (
        P(("req", "row"), "col"),
        P("col", "row", None),
        P("req", None, None),
        P("req", None, "row", None),
        P(),
        P(),
        P(),
        P(),
        P("req", "row", None, None),
        P(("req", "col"), "row"),
    )
    return jax.shard_map(
        functools.partial(body, mesh.shape["req"]),
        mesh=mesh,
        in_specs=placed,
        out_specs=P(("req", "col"), "row"),
        check_vma=False,
    )
```

```python
import functools
import math

import jax
import jax.numpy as jnp
from jax import lax
from jax.experimental import pallas as pl
from jax.experimental.pallas import tpu as pltpu
from jax.sharding import PartitionSpec as P

BLK = 64
NX = 4
NY = 4
MESH = pl.DeviceIdType.MESH
F32 = jnp.float32
BF16 = jnp.bfloat16


def kernel(
    n_req,
    row_ref,
    of_ref,
    len_ref,
    slot_ref,
    tok_ref,
    w_ref,
    a_ref,
    b_ref,
    state_ref,
    decay_ref,
    out_ref,
    tok,
    w,
    za,
    zb,
    xsa,
    xsb,
    xra,
    xrb,
    afull,
    bfull,
    bh,
    wtmp,
    wraw,
    wl,
    acc,
    sloc,
    ssend,
    states,
    dec,
    carry,
    osend,
    tok_s,
    tok_r,
    w_s,
    w_r,
    z_s,
    z_r,
    x_s,
    x_r,
    g_s,
    g_r,
    st_s,
    st_r,
    d_s,
    d_r,
    o_s,
    o_r,
    loc,
    up_sem,
    down_sem,
    side_sem,
):
    nz = n_req // NX
    g = lax.axis_index("req")
    r = lax.axis_index("row")
    c = lax.axis_index("col")
    z, x = g // NX, lax.rem(g, NX)
    sib = 1 - r
    right, left, opp = lax.rem(c + 1, NY), lax.rem(c + 3, NY), lax.rem(c + 2, NY)
    half = tok_ref.shape[0]
    part = half // 2
    base = r * half

    def rem_copy(src, dst, ssem, rsem, dev):
        return pltpu.make_async_remote_copy(
            src_ref=src, dst_ref=dst, send_sem=ssem, recv_sem=rsem, device_id=dev, device_id_type=MESH
        )

    def at_z(d):
        return {"req": lax.rem(z + d, nz) * NX + x}

    def at_x(d):
        return {"req": z * NX + lax.rem(x + d, NX)}

    def at_g(d):
        return {"req": lax.rem(g + d, n_req)}

    group = [(dr, dc) for dr in range(2) for dc in range(NY) if dr or dc]

    def in_group(dr, dc):
        return {"row": lax.rem(r + dr, 2), "col": lax.rem(c + dc, NY)}

    raw = pltpu.make_async_copy(w_ref, wraw, loc.at[7])
    raw.start()

    near = [in_group(*p) for p in group] + [at_z(1), at_z(nz - 1), at_x(1), at_x(NX - 1)]
    barrier = pltpu.get_barrier_semaphore()
    for dev in near:
        pl.semaphore_signal(barrier, inc=1, device_id=dev, device_id_type=MESH)
    pl.semaphore_wait(barrier, len(near))

    sends = []

    def send(src, dst, ssem, rsem, dev):
        cp = rem_copy(src, dst, ssem, rsem, dev)
        cp.start()
        sends.append(cp)

    def landed(slot, ssem, rsem, dev):
        rem_copy(slot, slot, ssem, rsem, dev).wait_recv()

    hrow = lax.rem(x, 2) * 128
    orow = 128 - hrow
    eighth = 64

    def wsend(i, src, dst, dev):
        send(src, dst, w_s.at[i], w_r.at[i], dev)

    def wwait(i, slot, dev):
        landed(slot, w_s.at[i], w_r.at[i], dev)

    mine_h = pl.ds(hrow, 128)
    first_h, second_h = pl.ds(hrow, eighth), pl.ds(hrow + eighth, eighth)
    first_o, second_o = pl.ds(orow, eighth), pl.ds(orow + eighth, eighth)

    def chunk(k):
        return pl.ds(base + k * part, part)

    def tsend(i, src, dst, dev):
        send(src, dst, tok_s.at[i], tok_r.at[i], dev)

    def twait(i, slot, dev):
        landed(slot, tok_s.at[i], tok_r.at[i], dev)

    def tok_chunk(k):
        return tok_ref.at[pl.ds(k * part, part)]

    tsend(0, tok_chunk(0), tok.at[c, chunk(0)], {"col": right})
    tsend(1, tok_chunk(1), tok.at[c, chunk(1)], {"col": left})
    tsend(4, tok_ref, tok.at[c, pl.ds(base, half)], {"row": sib})
    own_t = pltpu.make_async_copy(tok_ref, tok.at[c, pl.ds(base, half)], loc.at[3])
    own_t.start()
    own_s = pltpu.make_async_copy(state_ref.at[:, c], sloc, loc.at[6])
    own_s.start()

    def greet():
        pl.semaphore_signal(up_sem, inc=1, device_id=at_z(nz - 1), device_id_type=MESH)
        pl.semaphore_signal(down_sem, inc=1, device_id=at_z(1), device_id_type=MESH)

    greet()
    pl.semaphore_signal(side_sem, inc=1, device_id=at_x(NX - 1), device_id_type=MESH)

    raw.wait()

    def regroup(i, _):
        span = pl.ds(pl.multiple_of(32 * i, 32), 32)
        for h in range(NY):
            wl[h, span, :] = wraw[span, h, :]
        return 0

    lax.fori_loop(0, 8, regroup, 0)

    d_in = []
    for d in range(1, NY):
        to, frm = lax.rem(c + d, NY), lax.rem(c + NY - d, NY)
        send(decay_ref, dec.at[c], d_s.at[d], d_r.at[d], {"col": to})
        d_in.append((dec.at[frm], d_s.at[d], d_r.at[d], {"col": to}))
    own_d = pltpu.make_async_copy(decay_ref, dec.at[c], loc.at[4])
    own_d.start()

    wsend(0, wl.at[opp, first_h], wtmp.at[0], {"col": right})
    wsend(1, wl.at[opp, second_h], wtmp.at[1], {"col": left})
    wsend(2, wl.at[right, mine_h], w.at[c, mine_h], {"col": right})
    wsend(3, wl.at[left, mine_h], w.at[c, mine_h], {"col": left})
    own_w = pltpu.make_async_copy(wl.at[c], w.at[c], loc.at[2])
    own_w.start()

    pl.semaphore_wait(side_sem, 1)
    for step in range(3):
        if step > 0:
            greet()
        pl.semaphore_wait(up_sem, 1)
        pl.semaphore_wait(down_sem, 1)

    f = 2 * c + r
    fa = pl.multiple_of(f * 128, 128)
    mine_a = a_ref.at[:, :, pl.ds(fa, 128)]
    mine_b = b_ref.at[:, pl.ds(4 * c, 4)]
    z_in = []
    for d in (4, 3, 5, 2, 6, 1, 7):
        zo = lax.rem(z + nz - d, nz)
        for k, (src, dst) in enumerate(((mine_a, za), (mine_b, zb))):
            send(src, dst.at[pl.ds(2 * z, 2)], z_s.at[k, d], z_r.at[k, d], at_z(d))
            z_in.append((dst.at[pl.ds(2 * zo, 2)], z_s.at[k, d], z_r.at[k, d], at_z(d)))
    own_a = pltpu.make_async_copy(mine_a, za.at[pl.ds(2 * z, 2)], loc.at[0])
    own_b = pltpu.make_async_copy(mine_b, zb.at[pl.ds(2 * z, 2)], loc.at[1])
    own_a.start()
    own_b.start()

    own_s.wait()
    st_in = []
    for k, d in enumerate((1, n_req // 2)):
        taker = lax.rem(g + d, n_req)
        s0, s1 = slot_ref[2 * taker], slot_ref[2 * taker + 1]
        ssend[k] = sloc[lax.rem(jnp.where(s0 // 2 == g, s0, s1), 2)].astype(BF16)
    for k, d in enumerate((1, n_req // 2)):
        send(ssend.at[k], states.at[k], st_s.at[k], st_r.at[k], at_g(d))
        st_in.append((states.at[k], st_s.at[k], st_r.at[k], at_g(d)))

    wwait(0, wtmp.at[0], {"col": right})
    wsend(4, wtmp.at[0], w.at[left, first_h], {"col": right})
    tsend(2, tok_chunk(1), tok.at[c, chunk(1)], {"col": right})
    wwait(1, wtmp.at[1], {"col": left})
    wsend(5, wtmp.at[1], w.at[right, second_h], {"col": left})
    tsend(3, tok_chunk(0), tok.at[c, chunk(0)], {"col": left})

    for i, (frm, to) in enumerate(((left, right), (right, left))):
        wwait(2 + i, w.at[frm, mine_h], {"col": to})
        wsend(6 + 2 * i, w.at[frm, first_h], w.at[frm, first_h], at_x(1))
        wsend(7 + 2 * i, w.at[frm, second_h], w.at[frm, second_h], at_x(NX - 1))

    tile = 4 * BLK
    other = sib * half
    dev = {"row": sib}
    own_t.wait()
    own_w.wait()
    twait(4, tok.at[c, pl.ds(other, half)], dev)

    def share(q, fresh):
        def one(m, _):
            span = pl.ds(pl.multiple_of(m * tile, tile), tile)
            part_sum = jnp.dot(tok[q, span, :], w[q], preferred_element_type=F32)
            acc[span, :] = part_sum if fresh else acc[span, :] + part_sum
            return 0

        lax.fori_loop(0, NY, one, 0)

    share(c, True)

    slot_l0, slot_l1 = tok.at[left, chunk(0)], tok.at[left, chunk(1)]
    slot_r0, slot_r1 = tok.at[right, chunk(0)], tok.at[right, chunk(1)]
    slot_o0, slot_o1 = tok.at[opp, chunk(0)], tok.at[opp, chunk(1)]
    twait(0, slot_l0, {"col": right})
    tsend(5, slot_l0, slot_l0, {"col": right})
    tsend(6, slot_l0, slot_l0, {"row": sib})
    twait(1, slot_r1, {"col": left})
    tsend(7, slot_r1, slot_r1, {"col": left})
    tsend(8, slot_r1, slot_r1, {"row": sib})

    for got in z_in:
        landed(*got)
    own_a.wait()
    own_b.wait()
    for d in range(NX):
        gx = z * NX + lax.rem(x + d, NX)
        for j in range(2):
            p = row_ref[of_ref[j, gx]]
            idx = 2 * (p // (2 * NX)) + lax.rem(p, 2)
            if d == 0:
                xra[0, j] = za[idx]
                xrb[0, j] = zb[idx]
            else:
                xsa[d - 1, j] = za[idx]
                xsb[d - 1, j] = zb[idx]
    x_in = []
    for d in range(1, NX):
        for k, (src, dst) in enumerate(((xsa, xra), (xsb, xrb))):
            send(src.at[d - 1], dst.at[d], x_s.at[k, d], x_r.at[k, d], at_x(d))
            x_in.append((dst.at[d], x_s.at[k, d], x_r.at[k, d], at_x(d)))

    wwait(4, w.at[opp, first_h], {"col": right})
    wsend(10, w.at[opp, first_h], w.at[opp, first_h], at_x(1))
    wwait(5, w.at[opp, second_h], {"col": left})
    wsend(11, w.at[opp, second_h], w.at[opp, second_h], at_x(NX - 1))

    twait(2, slot_l1, {"col": right})
    tsend(9, slot_l1, slot_l1, {"row": sib})
    twait(3, slot_r0, {"col": left})
    tsend(10, slot_r0, slot_r0, {"row": sib})

    for got in x_in:
        landed(*got)
    for j in range(2):
        p = row_ref[of_ref[j, g]]
        xo = lax.rem(p // 2, NX)
        dd = lax.rem(x - xo + NX, NX)
        afull[pl.ds(16 * j, 16), pl.ds(fa, 128)] = xra[dd, j]
        bfull[j, pl.ds(4 * c, 4)] = xrb[dd, j]
    g_in = []
    ga = afull.at[:, pl.ds(fa, 128)]
    gb = bfull.at[:, pl.ds(4 * c, 4)]
    for i, (dr, dc) in enumerate(group):
        to = in_group(dr, dc)
        fc = lax.rem(c + NY - dc, NY)
        rf = 2 * fc + lax.rem(r + dr, 2)
        send(ga, ga, g_s.at[0, i], g_r.at[0, i], to)
        g_in.append((afull.at[:, pl.ds(pl.multiple_of(rf * 128, 128), 128)], g_s.at[0, i], g_r.at[0, i], to))
        if dr == 0:
            send(gb, gb, g_s.at[1, i], g_r.at[1, i], to)
            g_in.append((bfull.at[:, pl.ds(4 * fc, 4)], g_s.at[1, i], g_r.at[1, i], to))

    for i, (frm, to) in enumerate(((left, right), (right, left))):
        wwait(6 + 2 * i, w.at[frm, first_o], at_x(1))
        wwait(7 + 2 * i, w.at[frm, second_o], at_x(NX - 1))
    twait(6, tok.at[left, pl.ds(other, part)], dev)
    twait(9, tok.at[left, pl.ds(other + part, part)], dev)
    share(left, False)
    twait(10, tok.at[right, pl.ds(other, part)], dev)
    twait(8, tok.at[right, pl.ds(other + part, part)], dev)
    share(right, False)

    twait(5, slot_o0, {"col": right})
    tsend(11, slot_o0, slot_o0, {"row": sib})
    twait(7, slot_o1, {"col": left})
    tsend(12, slot_o1, slot_o1, {"row": sib})

    own_d.wait()
    for got in d_in + st_in + g_in:
        landed(*got)
    wwait(10, w.at[opp, first_o], at_x(1))
    wwait(11, w.at[opp, second_o], at_x(NX - 1))

    head_rows = lax.broadcasted_iota(jnp.int32, (4, 256), 0) == c
    for j in range(2):
        for k in range(16):
            row = jnp.sum(jnp.where(head_rows, bfull[j, k].astype(F32), 0.0), axis=0, keepdims=True)
            bh[pl.ds(16 * j + k, 1), :] = row

    first = len_ref[0, g]
    for j in range(2):
        s = slot_ref[2 * g + j]
        carry[j] = states[jnp.where(s // 2 == lax.rem(g + n_req - 1, n_req), 0, 1)].astype(F32)

    rows_i = lax.broadcasted_iota(jnp.int32, (tile, 1), 0)
    ti = lax.broadcasted_iota(jnp.int32, (tile, tile), 0)
    si = lax.broadcasted_iota(jnp.int32, (tile, tile), 1)
    seen = (ti // BLK == si // BLK) & (si <= ti)
    nt = (((1,), (1,)), ((), ()))
    tn = (((0,), (0,)), ((), ()))
    inv = 1.0 / math.sqrt(128.0)

    def one_tile(m, _):
        span = pl.ds(pl.multiple_of(m * tile, tile), tile)
        proj = acc[span, :] + jnp.dot(tok[opp, span, :], w[opp], preferred_element_type=F32)
        low = jnp.zeros((tile, 32), F32)
        for cc in range(NY):
            t = tok[cc, span, :]
            low += lax.dot_general(t, afull[:, cc * 256 : (cc + 1) * 256], nt, preferred_element_type=F32)
        request = (m * 4 + rows_i // BLK >= first).astype(jnp.int32)
        owner = lax.broadcasted_iota(jnp.int32, (tile, 32), 1) // 16
        low = jnp.where(owner == request, low, 0.0)
        hi = low.astype(BF16)
        lo = (low - hi.astype(F32)).astype(BF16)
        up = bh[...].astype(BF16)
        delta = jnp.dot(hi, up, preferred_element_type=F32) + jnp.dot(lo, up, preferred_element_type=F32)
        q = (proj[:, 0:128] + delta[:, 0:128]).astype(BF16)
        k = proj[:, 128:256].astype(BF16)
        v = (proj[:, 256:384] + delta[:, 128:256]).astype(BF16)
        gate = proj[:, 384:512].astype(BF16).astype(F32)
        qf, kf = q.astype(F32), k.astype(F32)
        sq = lax.rsqrt(jnp.mean(qf * qf, axis=1, keepdims=True) + 1e-06) * inv
        sk = lax.rsqrt(jnp.mean(kf * kf, axis=1, keepdims=True) + 1e-06) * inv
        vk = (v.astype(F32) * sk).astype(BF16)
        scores = lax.dot_general(q, k, nt, preferred_element_type=F32)
        scores = jnp.where(seen, scores, 0.0).astype(BF16)
        inner = jnp.dot(scores, vk, preferred_element_type=F32)
        dm = dec[m]
        fade = jnp.sum(
            jnp.where(lax.broadcasted_iota(jnp.int32, (4, 4), 1) == c, dm, 0.0), axis=1, keepdims=True
        )
        reads = []
        state = carry[0]
        for i in range(4):
            state = jnp.where(m * 4 + i == first, carry[1], state)
            sl = slice(i * BLK, (i + 1) * BLK)
            reads.append(jnp.dot(q[sl], state.astype(BF16), preferred_element_type=F32))
            upd = lax.dot_general(k[sl], vk[sl], tn, preferred_element_type=F32)
            state = state * fade[i : i + 1, :] + upd * (1.0 / BLK)
        carry[0] = state
        mem = (jnp.concatenate(reads, axis=0) + inner) * sq
        osend[m] = (mem * jax.nn.sigmoid(gate)).astype(BF16)

        place = out_ref.at[:, pl.ds(pl.multiple_of(c * 128, 128), 128)]

        @pl.when(m == c)
        def _():
            pltpu.make_async_copy(osend.at[m], place, loc.at[5]).start()

        @pl.when(m != c)
        def _():
            rem_copy(osend.at[m], place, o_s.at[m], o_r.at[c], {"col": m}).start()

        return 0

    twait(11, tok.at[opp, pl.ds(other, part)], dev)
    twait(12, tok.at[opp, pl.ds(other + part, part)], dev)
    lax.fori_loop(0, NY, one_tile, 0)

    for cp in sends:
        cp.wait_send()
    for d in range(1, NY):
        frm = lax.rem(c + d, NY)
        place = out_ref.at[:, pl.ds(pl.multiple_of(frm * 128, 128), 128)]
        cp = rem_copy(osend.at[frm], place, o_s.at[frm], o_r.at[frm], {"col": frm})
        cp.wait_send()
        cp.wait_recv()
    place = out_ref.at[:, pl.ds(pl.multiple_of(c * 128, 128), 128)]
    pltpu.make_async_copy(osend.at[c], place, loc.at[5]).wait()


def body(
    n_req, tokens, w_proj, adapter_a, adapter_b, adapter_row, adapter_of, len_blocks, state_slot, init_state, decay
):
    a_t = jnp.swapaxes(adapter_a, 1, 2)
    nz = n_req // NX
    dma = pltpu.SemaphoreType.DMA
    smem = pl.BlockSpec(memory_space=pltpu.SMEM)
    anym = pl.BlockSpec(memory_space=pl.ANY)
    return pl.pallas_call(
        functools.partial(kernel, n_req),
        out_shape=jax.ShapeDtypeStruct((256, 512), BF16),
        in_specs=[smem] * 4 + [anym] * 5 + [pl.BlockSpec(memory_space=pltpu.VMEM)],
        out_specs=anym,
        scratch_shapes=[
            pltpu.VMEM((NY, 1024, 256), BF16),
            pltpu.VMEM((NY, 256, 512), BF16),
            pltpu.VMEM((2 * nz, 16, 128), BF16),
            pltpu.VMEM((2 * nz, 4, 4, 256), BF16),
            pltpu.VMEM((NX - 1, 2, 16, 128), BF16),
            pltpu.VMEM((NX - 1, 2, 4, 4, 256), BF16),
            pltpu.VMEM((NX, 2, 16, 128), BF16),
            pltpu.VMEM((NX, 2, 4, 4, 256), BF16),
            pltpu.VMEM((32, 1024), BF16),
            pltpu.VMEM((2, 16, 4, 256), BF16),
            pltpu.VMEM((32, 256), F32),
            pltpu.VMEM((2, 64, 512), BF16),
            pltpu.VMEM((256, NY, 512), BF16),
            pltpu.VMEM((NY, 256, 512), BF16),
            pltpu.VMEM((1024, 512), F32),
            pltpu.VMEM((2, 128, 128), F32),
            pltpu.VMEM((2, 128, 128), BF16),
            pltpu.VMEM((2, 128, 128), BF16),
            pltpu.VMEM((NY, 4, 4), F32),
            pltpu.VMEM((2, 128, 128), F32),
            pltpu.VMEM((NY, 256, 128), BF16),
            dma((13,)),
            dma((13,)),
            dma((12,)),
            dma((12,)),
            dma((2, nz)),
            dma((2, nz)),
            dma((2, NX)),
            dma((2, NX)),
            dma((2, 7)),
            dma((2, 7)),
            dma((2,)),
            dma((2,)),
            dma((NY,)),
            dma((NY,)),
            dma((NY,)),
            dma((NY,)),
            dma((8,)),
            pltpu.SemaphoreType.REGULAR,
            pltpu.SemaphoreType.REGULAR,
            pltpu.SemaphoreType.REGULAR,
        ],
        compiler_params=pltpu.CompilerParams(collective_id=0, has_side_effects=True),
        name="memory_layer",
    )(
        adapter_row,
        jnp.transpose(adapter_of),
        jnp.transpose(len_blocks),
        state_slot,
        tokens,
        w_proj,
        a_t,
        adapter_b,
        init_state,
        decay,
    )


def solution(mesh):
    placed = (
        P(("req", "row"), "col"),
        P("col", "row", None),
        P("req", None, None),
        P("req", None, "row", None),
        P(),
        P(),
        P(),
        P(),
        P("req", "row", None, None),
        P(("req", "col"), "row"),
    )
    return jax.shard_map(
        functools.partial(body, mesh.shape["req"]),
        mesh=mesh,
        in_specs=placed,
        out_specs=P(("req", "col"), "row"),
        check_vma=False,
    )
```
